128 devices in a mesh: gz: 8 (over z, y_hi), gx: 16 (over x, y_lo, core).
Axes of the slice: x: 4, y: 4 (y_hi: 2, y_lo: 2; y = y_hi * 2 + y_lo), z: 4, core: 2. Of those that a mesh axis runs over, the one named last changes fastest.
Arguments:
- strain: float32 [6, 2, 1024, 1024], P(None, None, 'gx', 'gz'), may hold values from -6 to 6
- labels: int32 [2, 1024, 1024], P(None, 'gx', 'gz'), may hold values 0 or 1
- normals: int32 [2, 64, 64], P(None, 'gx', 'gz'), may hold values from 0 to 7
- moduli: float32 [5], replicated, may hold values from 0.5 to 4
- mean_strain: float32 [6], replicated, may hold values from -4 to 4
Outputs:
- strain_next: float32 [6, 2, 1024, 1024], P(None, None, 'gx', 'gz')
- stress_next: float32 [6, 2, 1024, 1024], P(None, None, 'gx', 'gz')
The draws below stay inside these ranges and needn't reach their ends.
All inputs are finite; a program needn't handle non-finite values. No bound on the sum of `labels` on one device may be relied on, other than what follows from the above.
Results may differ from the reference program's by a relative error of at most 0.000082.
Values sent between devices are 32-bit elements; how exact they have to be, the bound alone decides.
A program may use at most 128 MiB of HBM per device.

```python
import math
import jax
import jax.numpy as jnp
from jax import lax

NX = 1024
NZ = 1024
SECTIONS = 2
ANGLES = 8
BLK = 16


def place_ends(values, rng, low, top_value):
    longest = values.shape.index(max(values.shape))
    spots = []
    for shift in (0, 1):
        where = [jax.random.randint(jax.random.fold_in(rng, axis), (), 0, length) for axis, length in enumerate(values.shape)]
        where[longest] = (where[longest] + shift) % values.shape[longest]
        spots.append(tuple(where))
    return values.at[spots[0]].set(low).at[spots[1]].set(top_value)


def steps_of(stream_key, shape, shards, low, high):
    loudness, own = 1.0, jax.random.fold_in(stream_key, 6)
    for dim, shards_of in shards:
        heights = jnp.exp(jax.random.uniform(jax.random.fold_in(own, dim), (shards_of,), jnp.float32, low / len(shards), high / len(shards)))
        loudness = loudness * jnp.repeat(heights, shape[dim] // shards_of).reshape([-1 if axis == dim else 1 for axis in range(len(shape))])
    return loudness


def normal_values(key, shape, deviation, bound, split=(), kind=jnp.bfloat16):
    entries = jax.random.normal(key, shape, jnp.float32) * deviation
    if len(split) > 0:
        entries = steps_of(key, shape, split, -0.22, 0.18) * entries
    return jnp.clip(entries, min=-bound, max=bound).astype(kind)


def setup_inputs(seed: int = 0) -> dict:
    seeds = jax.random.split(jax.random.key(seed), 6)
    strain = normal_values(seeds[0], (6, SECTIONS, NX, NZ), 1.0, 6.0, ((2, 16), (3, 8)), jnp.float32)
    labels = place_ends((jax.random.randint(seeds[1], (SECTIONS, NX, NZ), 0, 5) < 2).astype(jnp.int32), jax.random.fold_in(seeds[1], 1), 0, 1)
    normals = place_ends(jax.random.randint(seeds[2], (SECTIONS, NX // BLK, NZ // BLK), 0, ANGLES), jax.random.fold_in(seeds[2], 1), 0, ANGLES - 1).astype(jnp.int32)
    moduli = jnp.clip(jnp.exp(jax.random.uniform(seeds[3], (5,), jnp.float32, math.log(0.5), math.log(4.0))), 0.5, 4.0)
    mean_strain = normal_values(seeds[4], (6,), 1.0, 4.0, (), jnp.float32)
    return dict(strain=strain, labels=labels, normals=normals, moduli=moduli, mean_strain=mean_strain)


def orientation(normals):
    tilt_angle = math.pi / ANGLES * normals.astype(jnp.float32)
    tilt_angle = jnp.repeat(jnp.repeat(tilt_angle, BLK, axis=1), BLK, axis=2)
    return (jnp.cos(tilt_angle), jnp.sin(tilt_angle))

def stress_law(strain_field, labels, cosine_tilt, sine_tilt, moduli):
    laminate = labels == 1
    lame_local = jnp.where(laminate, moduli[2], moduli[0])
    shear_local = jnp.where(laminate, moduli[3], moduli[1])
    trace_sum = strain_field[0] + strain_field[1] + strain_field[2]
    normal_part = cosine_tilt * cosine_tilt * strain_field[0] + sine_tilt * sine_tilt * strain_field[2] + 2.0 * cosine_tilt * sine_tilt * strain_field[4]
    laminate_term = moduli[4] * labels.astype(jnp.float32) * normal_part
    dyad = [cosine_tilt * cosine_tilt, None, sine_tilt * sine_tilt, None, cosine_tilt * sine_tilt, None]
    result = []
    for slot in range(6):
        value = 2.0 * shear_local * strain_field[slot]
        if slot < 3:
            value = value + lame_local * trace_sum
        if dyad[slot] is not None:
            value = value + laminate_term * dyad[slot]
        result.append(value)
    return jnp.stack(result)

def polarize(stresses, strain_field, lame_ref, shear_ref):
    trace_sum = strain_field[0] + strain_field[1] + strain_field[2]
    result = []
    for slot in range(6):
        value = stresses[slot] - 2.0 * shear_ref * strain_field[slot]
        if slot < 3:
            value = value - lame_ref * trace_sum
        result.append(value)
    return jnp.stack(result)

def green_apply(spectrum, unit_x, unit_z, lame_ref, shear_ref):
    coupling = (lame_ref + shear_ref) / (shear_ref * (lame_ref + 2.0 * shear_ref))
    traction_x = spectrum[0] * unit_x + spectrum[4] * unit_z
    traction_y = spectrum[5] * unit_x + spectrum[3] * unit_z
    traction_z = spectrum[4] * unit_x + spectrum[2] * unit_z
    normal_load = unit_x * traction_x + unit_z * traction_z
    half_inverse = 0.5 / shear_ref
    result = [2.0 * half_inverse * unit_x * traction_x - coupling * normal_load * unit_x * unit_x, jnp.zeros_like(traction_x), 2.0 * half_inverse * unit_z * traction_z - coupling * normal_load * unit_z * unit_z, half_inverse * unit_z * traction_y, half_inverse * (unit_z * traction_x + unit_x * traction_z) - coupling * normal_load * unit_x * unit_z, half_inverse * unit_x * traction_y]
    return -jnp.stack(result)

def signed_freq(length):
    counter = jnp.arange(length, dtype=jnp.int32)
    return jnp.where(counter < length // 2, counter, counter - length).astype(jnp.float32)

def reference(strain, labels, normals, moduli, mean_strain):
    cosine_tilt, sine_tilt = orientation(normals)
    lame_ref = 0.5 * (moduli[0] + moduli[2])
    shear_ref = 0.5 * (moduli[1] + moduli[3])
    stresses = stress_law(strain, labels, cosine_tilt, sine_tilt, moduli)
    polarized = polarize(stresses, strain, lame_ref, shear_ref)
    freq_x = signed_freq(NX)[:, None]
    freq_z = signed_freq(NZ)[None, :]
    radius_sq = freq_x * freq_x + freq_z * freq_z
    at_anchor = radius_sq == 0.0
    safe_radius = jnp.sqrt(jnp.where(at_anchor, 1.0, radius_sq))
    unit_x = freq_x / safe_radius
    unit_z = freq_z / safe_radius
    anchor_term = jnp.where(at_anchor, float(NX * NZ), 0.0)

    def one_section(section_index):
        part_field = lax.dynamic_index_in_dim(polarized, section_index, 1, keepdims=False)
        spectrum = jnp.fft.fft2(part_field, axes=(1, 2))
        real_part = green_apply(spectrum.real, unit_x, unit_z, lame_ref, shear_ref)
        real_part = real_part + mean_strain[:, None, None] * anchor_term[None]
        imag_part = green_apply(spectrum.imag, unit_x, unit_z, lame_ref, shear_ref)
        inverse = jnp.fft.ifft2(real_part + 1j * imag_part, axes=(1, 2)).real
        return inverse.astype(jnp.float32)
    sections_out = lax.map(one_section, jnp.arange(SECTIONS, dtype=jnp.int32))
    strain_next = jnp.moveaxis(sections_out, 0, 1)
    stress_next = stress_law(strain_next, labels, cosine_tilt, sine_tilt, moduli)
    return (strain_next, stress_next)
```

```python
import functools
import math

import jax
import jax.numpy as jnp
import numpy as np
from jax import lax
from jax.experimental import pallas as pl
from jax.experimental.pallas import tpu as pltpu
from jax.sharding import PartitionSpec as P

ANGLES = 8
BLK = 16
COMPS = (0, 2, 4, 3, 5)
MESH = pl.DeviceIdType.MESH
HIGH = lax.Precision.HIGHEST
ROOT = math.sqrt(0.5)


def tables():
    k = np.arange(128)
    w = 2.0 * np.pi / 128.0 * (k[:, None] * k[None, :] % 128)
    dft = np.concatenate([np.cos(w), np.sin(w)], axis=1)
    r = np.arange(8)
    wz = 2.0 * np.pi / 1024.0 * (r[:, None] * k[None, :])
    twz = np.concatenate([np.cos(wz), np.sin(wz)], axis=0)
    lane = np.arange(128)
    t, low = lane // 64, lane % 8
    wx = 2.0 * np.pi / 1024.0 * (k[:, None] * low[None, :])
    sign = np.where(t == 0, 1.0, -1.0)[None, :]
    twx = np.concatenate([np.cos(wx), np.sin(wx) * sign], axis=0)
    same = (lane // 8 % 8)[:, None] == (lane // 8 % 8)[None, :]
    w8 = 2.0 * np.pi / 8.0 * (low[:, None] * low[None, :] % 8)
    ta, tb = t[:, None], t[None, :]
    cos8, sin8 = np.cos(w8) * same, np.sin(w8) * same
    fwd = np.where(ta == tb, cos8, np.where(ta == 1, sin8, -sin8))
    inv = np.where(ta == tb, cos8, np.where(ta == 1, -sin8, sin8))
    fwd2 = np.concatenate([fwd, np.roll(fwd, 64, axis=0)], axis=0)
    inv2 = np.concatenate([inv, np.roll(inv, 64, axis=1)], axis=1)
    return [np.asarray(a, np.float32) for a in (dft, twz, twx, fwd2, inv2)]


def dot(a, b, ca=1, cb=0):
    return lax.dot_general(
        a, b, (((ca,), (cb,)), ((), ())), precision=HIGH, preferred_element_type=jnp.float32
    )


def fft8(u, sign):
    def add(a, b):
        return (a[0] + b[0], a[1] + b[1])

    def sub(a, b):
        return (a[0] - b[0], a[1] - b[1])

    def turn(a):
        return (-a[1], a[0]) if sign > 0 else (a[1], -a[0])

    def fft4(v):
        e, f = add(v[0], v[2]), sub(v[0], v[2])
        g, h = add(v[1], v[3]), turn(sub(v[1], v[3]))
        return [add(e, g), add(f, h), sub(e, g), sub(f, h)]

    even, odd = fft4(u[0::2]), fft4(u[1::2])
    o1, o3 = odd[1], odd[3]
    t1, t3 = turn(o1), turn(o3)
    odd = [
        odd[0],
        ((o1[0] + t1[0]) * ROOT, (o1[1] + t1[1]) * ROOT),
        turn(odd[2]),
        ((t3[0] - o3[0]) * ROOT, (t3[1] - o3[1]) * ROOT),
    ]
    return [add(even[k], odd[k]) for k in range(4)] + [sub(even[k], odd[k]) for k in range(4)]


def z_forward(load, twz):
    blocks = []
    for c in range(5):
        u = fft8([(load(j, 2 * c), load(j, 2 * c + 1)) for j in range(8)], -1)
        real, imag = [], []
        for r in range(8):
            re, im = u[r]
            if r:
                co, si = twz[r : r + 1, :], twz[8 + r : 9 + r, :]
                re, im = re * co + im * si, im * co - re * si
            real.append(re)
            imag.append(im)
        re, im = jnp.concatenate(real, axis=0), jnp.concatenate(imag, axis=0)
        left = jnp.concatenate([re, im], axis=0)
        right = jnp.concatenate([im, -re], axis=0)
        blocks.append(jnp.concatenate([left, right], axis=1))
    return blocks


def z_inverse(parts, twz):
    v = []
    for r in range(8):
        lo, hi = slice(8 * r, 8 * r + 8), slice(64 + 8 * r, 72 + 8 * r)
        re = parts[lo, :128] - parts[hi, 128:]
        im = parts[hi, :128] + parts[lo, 128:]
        if r:
            co, si = twz[r : r + 1, :], twz[8 + r : 9 + r, :]
            re, im = re * co - im * si, im * co + re * si
        v.append((re, im))
    return fft8(v, 1)


def green(spec, kz_base, half, couple):
    row = lax.broadcasted_iota(jnp.int32, (128, 128), 0)
    lane = lax.broadcasted_iota(jnp.int32, (128, 128), 1)
    kx = row + 128 * (lane % 8)
    kz = kz_base + lane // 8 % 8
    fx = jnp.where(kx < 512, kx, kx - 1024).astype(jnp.float32)
    fz = jnp.where(kz < 512, kz, kz - 1024).astype(jnp.float32)
    xx, zz, xz = fx * fx, fz * fz, fx * fz
    size = xx + zz
    inv = 1.0 / jnp.where(size == 0.0, 1.0, size)
    p, q, r = xx * inv, zz * inv, xz * inv
    r = jnp.where((kx == 512) != (kz == 512), 0.0, r)
    s0, s2, s4, s3, s5 = spec
    even = s0 * p + s2 * q
    load = couple * (even + 2.0 * (s4 * r))
    return (
        2.0 * half * (s0 * p + s4 * r) - load * p,
        2.0 * half * (s2 * q + s4 * r) - load * q,
        half * (r * (s0 + s2) + s4 * (p + q)) - couple * (r * even + 2.0 * (s4 * (p * q))),
        half * (s5 * r + s3 * q),
        half * (s5 * p + s3 * r),
    )


def middle(rows, kz_base, half, couple, dft, twx, fwd2, inv2):
    lane = lax.broadcasted_iota(jnp.int32, (128, 128), 1)
    sign = jnp.where(lane < 64, 1.0, -1.0)
    cx, sx = twx[:128, :], twx[128:, :]
    spec = []
    for x in rows:
        other = swap(x) * sign
        x1 = dot(dft, jnp.concatenate([x, other], axis=0))
        spec.append(dot(jnp.concatenate([x1 * cx, -(x1 * sx)], axis=1), fwd2))
    out = []
    for new in green(spec, kz_base, half, couple):
        both = dot(new, inv2)
        y, ry = both[:, :128], both[:, 128:]
        y2 = y * cx - ry * sx
        ry2 = ry * cx + y * sx
        out.append(dot(dft, jnp.concatenate([y2, -(ry2 * sign)], axis=0)))
    return out


def swap(x):
    return pltpu.roll(x, 64, axis=1)


def stress_terms(moduli, labels):
    lam = jnp.where(labels == 1, moduli[2], moduli[0])
    mu = jnp.where(labels == 1, moduli[3], moduli[1])
    stiff = moduli[4] * labels.astype(jnp.float32)
    return lam, mu, stiff


def orient(normals, s):
    steps = normals.astype(jnp.float32)
    rows = lax.broadcasted_iota(jnp.int32, (64, 4), 0) // BLK == lax.broadcasted_iota(jnp.int32, (64, 4), 1)
    cols = lax.broadcasted_iota(jnp.int32, (8, 128), 0) == lax.broadcasted_iota(jnp.int32, (8, 128), 1) // BLK
    wide = dot(dot(rows.astype(jnp.float32), steps), cols.astype(jnp.float32))
    cosine, sine = jnp.ones_like(wide), jnp.zeros_like(wide)
    for k in range(1, ANGLES):
        here = jnp.abs(wide - k) < 0.5
        cosine = jnp.where(here, math.cos(math.pi / ANGLES * k), cosine)
        sine = jnp.where(here, math.sin(math.pi / ANGLES * k), sine)
    return cosine * cosine, sine * sine, cosine * sine


def law(e, lam, mu2, stiff, angle):
    cc, ss, cs = angle
    trace = lam * (e[0] + e[1] + e[2])
    normal = stiff * (cc * e[0] + ss * e[2] + 2.0 * cs * e[4])
    dyad = (cc, None, ss, None, cs, None)
    out = []
    for k in range(6):
        value = mu2 * e[k]
        if k < 3:
            value = value + trace
        if dyad[k] is not None:
            value = value + normal * dyad[k]
        out.append(value)
    return out


def kernel(
    zs, xs,
    moduli, mean, strain, labels, normals, dft_ref, twz_ref, twx_ref, fwd_ref, inv_ref,
    strain_out, stress_out,
    s1, r1, s2, r2, s3, r3, s4, r4,
    send, recv, ready,
):
    j = lax.axis_index("gz")
    i = lax.axis_index("gx")
    total = zs * xs
    me = zs * i + j

    barrier = pltpu.get_barrier_semaphore()
    for k in range(1, zs):
        pl.semaphore_signal(barrier, inc=1, device_id={"gz": lax.rem(j + k, zs), "gx": i}, device_id_type=MESH)
    for k in range(1, xs):
        pl.semaphore_signal(barrier, inc=1, device_id={"gz": j, "gx": lax.rem(i + k, xs)}, device_id_type=MESH)

    m = [moduli[k] for k in range(5)]
    lame_ref = 0.5 * (m[0] + m[2])
    shear_ref = 0.5 * (m[1] + m[3])
    for s in range(2):
        angle = orient(normals[s], s)
        lam, mu, stiff = stress_terms(m, labels[s])
        e = [strain[c, s] for c in range(6)]
        pol = law(e, lam - lame_ref, 2.0 * (mu - shear_ref), stiff, angle)
        for slot, c in enumerate(COMPS):
            for g in range(8):
                s1[g, 2 * slot + s] = pol[c][8 * g : 8 * g + 8, :]

    pl.semaphore_wait(barrier, zs + xs - 2)
    for k in range(1, xs):
        pl.semaphore_signal(ready, inc=1, device_id={"gz": j, "gx": lax.rem(i + k, xs)}, device_id_type=MESH)

    def z_exchange(src, dst, n):
        for k in range(1, zs):
            to = lax.rem(j + k, zs)
            pltpu.make_async_remote_copy(
                src_ref=src.at[to], dst_ref=dst.at[j], send_sem=send.at[n], recv_sem=recv.at[n],
                device_id={"gz": to, "gx": i}, device_id_type=MESH,
            ).start()
        dst[j] = src[j]
        pltpu.make_async_copy(dst.at[pl.ds(0, zs - 1)], dst.at[pl.ds(0, zs - 1)], recv.at[n]).wait()

    def all_exchange(src, dst, n):
        mine = pl.multiple_of(me * 8, 8)

        def step(k, carry):
            to = lax.rem(me + k, total)
            there = pl.multiple_of(to * 8, 8)
            pltpu.make_async_remote_copy(
                src_ref=src.at[pl.ds(there, 8), :], dst_ref=dst.at[pl.ds(mine, 8), :],
                send_sem=send.at[n], recv_sem=recv.at[n],
                device_id={"gz": lax.rem(to, zs), "gx": to // zs}, device_id_type=MESH,
            ).start()
            return carry

        lax.fori_loop(1, total, step, 0)
        dst[pl.ds(mine, 8), :] = src[pl.ds(mine, 8), :]
        rest = dst.at[pl.ds(0, 8 * (total - 1)), :]
        pltpu.make_async_copy(rest, rest, recv.at[n]).wait()

    z_exchange(s1, r1, 0)
    dft = dft_ref[...]
    twz = twz_ref[...]
    for c, block in enumerate(z_forward(lambda a, b: r1[a, b], twz)):
        s2[pl.ds(c, 128, stride=8), :] = dot(dft, block, 1, 1)

    pl.semaphore_wait(ready, xs - 1)
    all_exchange(s2, r2, 1)
    scale = -1.0 / (1024.0 * 1024.0)
    half = scale * 0.5 / shear_ref
    couple = scale * (lame_ref + shear_ref) / (shear_ref * (lame_ref + 2.0 * shear_ref))
    rows = [r2[pl.ds(c, 128, stride=8), :] for c in range(5)]
    out = middle(rows, 8 * me, half, couple, dft, twx_ref[...], fwd_ref[...], inv_ref[...])
    for c in range(5):
        s3[pl.ds(c, 128, stride=8), :] = out[c]

    all_exchange(s3, r3, 2)
    for c in range(5):
        w = r3[pl.ds(c, 128, stride=8), :]
        tiles = z_inverse(dot(w.T, dft), twz)
        for g in range(8):
            s4[g, 2 * c] = tiles[g][0]
            s4[g, 2 * c + 1] = tiles[g][1]

    z_exchange(s4, r4, 3)
    for s in range(2):
        angle = orient(normals[s], s)
        lam, mu, stiff = stress_terms(m, labels[s])
        e = [None] * 6
        for slot, c in enumerate(COMPS):
            e[c] = jnp.concatenate([r4[g, 2 * slot + s] for g in range(8)], axis=0) + mean[c]
        e[1] = jnp.full((64, 128), mean[1], jnp.float32)
        stress = law(e, lam, 2.0 * mu, stiff, angle)
        for c in range(6):
            strain_out[c, s] = e[c]
            stress_out[c, s] = stress[c]

    for n, ref in ((0, s1), (3, s4)):
        part = ref.at[pl.ds(0, zs - 1)]
        pltpu.make_async_copy(part, part, send.at[n]).wait()
    for n, ref in ((1, s2), (2, s3)):
        part = ref.at[pl.ds(0, 8 * (total - 1)), :]
        pltpu.make_async_copy(part, part, send.at[n]).wait()


def solution(mesh):
    zs, xs = mesh.shape["gz"], mesh.shape["gx"]
    consts = tables()

    def shards(strain, labels, normals, moduli, mean_strain):
        vmem = pl.BlockSpec(memory_space=pltpu.VMEM)
        smem = pl.BlockSpec(memory_space=pltpu.SMEM)
        tile = pltpu.VMEM((8, 10, 8, 128), jnp.float32)
        wide = pltpu.VMEM((1024, 128), jnp.float32)
        return tuple(
            pl.pallas_call(
                functools.partial(kernel, zs, xs),
                out_shape=[jax.ShapeDtypeStruct(strain.shape, jnp.float32)] * 2,
                in_specs=[smem, smem] + [vmem] * 8,
                out_specs=[vmem, vmem],
                scratch_shapes=[tile, tile, wide, wide, wide, wide, tile, tile]
                + [pltpu.SemaphoreType.DMA((4,)), pltpu.SemaphoreType.DMA((4,)), pltpu.SemaphoreType.REGULAR],
                compiler_params=pltpu.CompilerParams(collective_id=0, has_side_effects=True),
            )(moduli, mean_strain, strain, labels, normals, *[jnp.asarray(a) for a in consts])
        )

    in_specs = (P(None, None, "gx", "gz"), P(None, "gx", "gz"), P(None, "gx", "gz"), P(), P())
    out_specs = (P(None, None, "gx", "gz"), P(None, None, "gx", "gz"))
    return jax.shard_map(shards, mesh=mesh, in_specs=in_specs, out_specs=out_specs, check_vma=False)
```

```python
import itertools
import math

import jax
import jax.numpy as jnp
import numpy as np
from jax import lax
from jax.experimental import pallas as pl
from jax.experimental.pallas import tpu as pltpu
from jax.sharding import PartitionSpec as P

ANGLES = 8
BLK = 16
COMPS = (0, 2, 4, 3, 5)
MESH = pl.DeviceIdType.MESH
HIGH = lax.Precision.HIGHEST
ROOT = math.sqrt(0.5)


def tables():
    k = np.arange(128)
    w = 2.0 * np.pi / 128.0 * (k[:, None] * k[None, :] % 128)
    dft = np.concatenate([np.cos(w), np.sin(w)], axis=1)
    r = np.arange(8)
    wz = 2.0 * np.pi / 1024.0 * (r[:, None] * k[None, :])
    twz = np.concatenate([np.cos(wz), np.sin(wz)], axis=0)
    lane = np.arange(128)
    t, low = lane // 64, lane % 8
    wx = 2.0 * np.pi / 1024.0 * (k[:, None] * low[None, :])
    sign = np.where(t == 0, 1.0, -1.0)[None, :]
    twx = np.concatenate([np.cos(wx), np.sin(wx) * sign], axis=0)
    same = (lane // 8 % 8)[:, None] == (lane // 8 % 8)[None, :]
    w8 = 2.0 * np.pi / 8.0 * (low[:, None] * low[None, :] % 8)
    ta, tb = t[:, None], t[None, :]
    cos8, sin8 = np.cos(w8) * same, np.sin(w8) * same
    fwd = np.where(ta == tb, cos8, np.where(ta == 1, sin8, -sin8))
    inv = np.where(ta == tb, cos8, np.where(ta == 1, -sin8, sin8))
    fwd2 = np.concatenate([fwd, np.roll(fwd, 64, axis=0)], axis=0)
    inv2 = np.concatenate([inv, np.roll(inv, 64, axis=1)], axis=1)
    twz, twx = np.asarray(twz, np.float32), np.asarray(twx, np.float32)
    return [left_table(dft), right_table(dft), right_table(fwd2), right_table(inv2), twz, twx]


def halves(a):
    a = np.asarray(a, np.float32)
    high = a.astype(jnp.bfloat16)
    return high, (a - high.astype(np.float32)).astype(jnp.bfloat16)


def left_table(a):
    high, low = halves(a)
    return np.concatenate([high, low, high], axis=1)


def right_table(a):
    high, low = halves(a)
    return np.concatenate([high, low, high], axis=0)


def split3(x, axis):
    high = x.astype(jnp.bfloat16)
    low = (x - high.astype(jnp.float32)).astype(jnp.bfloat16)
    return jnp.concatenate([high, high, low], axis=axis)


def mul(a, b, ca=1, cb=0):
    return lax.dot_general(a, b, (((ca,), (cb,)), ((), ())), preferred_element_type=jnp.float32)


def dot(a, b):
    return lax.dot_general(
        a, b, (((1,), (0,)), ((), ())), precision=HIGH, preferred_element_type=jnp.float32
    )


def fft8(u, sign):
    def add(a, b):
        return (a[0] + b[0], a[1] + b[1])

    def sub(a, b):
        return (a[0] - b[0], a[1] - b[1])

    def turn(a):
        return (-a[1], a[0]) if sign > 0 else (a[1], -a[0])

    def fft4(v):
        e, f = add(v[0], v[2]), sub(v[0], v[2])
        g, h = add(v[1], v[3]), turn(sub(v[1], v[3]))
        return [add(e, g), add(f, h), sub(e, g), sub(f, h)]

    even, odd = fft4(u[0::2]), fft4(u[1::2])
    o1, o3 = odd[1], odd[3]
    t1, t3 = turn(o1), turn(o3)
    odd = [
        odd[0],
        ((o1[0] + t1[0]) * ROOT, (o1[1] + t1[1]) * ROOT),
        turn(odd[2]),
        ((t3[0] - o3[0]) * ROOT, (t3[1] - o3[1]) * ROOT),
    ]
    return [add(even[k], odd[k]) for k in range(4)] + [sub(even[k], odd[k]) for k in range(4)]


def z_forward(load, twz):
    blocks = []
    for c in range(5):
        u = fft8([(load(j, 2 * c), load(j, 2 * c + 1)) for j in range(8)], -1)
        real, imag = [], []
        for r in range(8):
            re, im = u[r]
            if r:
                co, si = twz[r : r + 1, :], twz[8 + r : 9 + r, :]
                re, im = re * co + im * si, im * co - re * si
            real.append(re)
            imag.append(im)
        re, im = jnp.concatenate(real, axis=0), jnp.concatenate(imag, axis=0)
        left = jnp.concatenate([re, im], axis=0)
        right = jnp.concatenate([im, -re], axis=0)
        blocks.append(jnp.concatenate([left, right], axis=1))
    return jnp.concatenate(blocks, axis=0)


def z_inverse(parts, twz):
    v = []
    for r in range(8):
        lo, hi = slice(8 * r, 8 * r + 8), slice(64 + 8 * r, 72 + 8 * r)
        re = parts[lo, :128] - parts[hi, 128:]
        im = parts[hi, :128] + parts[lo, 128:]
        if r:
            co, si = twz[r : r + 1, :], twz[8 + r : 9 + r, :]
            re, im = re * co - im * si, im * co + re * si
        v.append((re, im))
    return fft8(v, 1)


def green(spec, kz_base, half, couple):
    row = lax.broadcasted_iota(jnp.int32, (128, 128), 0)
    lane = lax.broadcasted_iota(jnp.int32, (128, 128), 1)
    kx = row + 128 * (lane % 8)
    kz = kz_base + lane // 8 % 8
    fx = jnp.where(kx < 512, kx, kx - 1024).astype(jnp.float32)
    fz = jnp.where(kz < 512, kz, kz - 1024).astype(jnp.float32)
    xx, zz, xz = fx * fx, fz * fz, fx * fz
    size = xx + zz
    inv = 1.0 / jnp.where(size == 0.0, 1.0, size)
    p, q, r = xx * inv, zz * inv, xz * inv
    r = jnp.where((kx == 512) != (kz == 512), 0.0, r)
    s0, s2, s4, s3, s5 = spec
    even = s0 * p + s2 * q
    load = couple * (even + 2.0 * (s4 * r))
    return (
        2.0 * half * (s0 * p + s4 * r) - load * p,
        2.0 * half * (s2 * q + s4 * r) - load * q,
        half * (r * (s0 + s2) + s4 * (p + q)) - couple * (r * even + 2.0 * (s4 * (p * q))),
        half * (s5 * r + s3 * q),
        half * (s5 * p + s3 * r),
    )


def middle(wide, kz_base, half, couple, tabs):
    left, _, fwd, inv, _, twx = tabs
    n = len(COMPS)
    lane = lax.broadcasted_iota(jnp.int32, (128, 128), 1)
    sign = jnp.where(lane < 64, 1.0, -1.0)
    cx, sx = twx[:128, :], twx[128:, :]

    def lanes(x, c):
        return x[:, 128 * c : 128 * c + 128]

    def rows(x, c):
        return x[128 * c : 128 * c + 128]

    pairs = [jnp.concatenate([lanes(wide, c), swap(lanes(wide, c)) * sign], axis=0) for c in range(n)]
    x1 = mul(left, split3(jnp.concatenate(pairs, axis=1), 0))
    turned = [jnp.concatenate([lanes(x1, c) * cx, -(lanes(x1, c) * sx)], axis=1) for c in range(n)]
    spec = mul(split3(jnp.concatenate(turned, axis=0), 1), fwd)
    new = green([rows(spec, c) for c in range(n)], kz_base, half, couple)
    both = mul(split3(jnp.concatenate(new, axis=0), 1), inv)
    out = []
    for c in range(n):
        y, ry = rows(both, c)[:, :128], rows(both, c)[:, 128:]
        out.append(jnp.concatenate([y * cx - ry * sx, -((ry * cx + y * sx) * sign)], axis=0))
    return mul(left, split3(jnp.concatenate(out, axis=1), 0))


def swap(x):
    return pltpu.roll(x, 64, axis=1)


def stress_terms(moduli, labels):
    lam = jnp.where(labels == 1, moduli[2], moduli[0])
    mu = jnp.where(labels == 1, moduli[3], moduli[1])
    stiff = moduli[4] * labels.astype(jnp.float32)
    return lam, mu, stiff


def orient(normals, s):
    steps = normals.astype(jnp.float32)
    rows = lax.broadcasted_iota(jnp.int32, (64, 4), 0) // BLK == lax.broadcasted_iota(jnp.int32, (64, 4), 1)
    cols = lax.broadcasted_iota(jnp.int32, (8, 128), 0) == lax.broadcasted_iota(jnp.int32, (8, 128), 1) // BLK
    wide = dot(dot(rows.astype(jnp.float32), steps), cols.astype(jnp.float32))
    cosine, sine = jnp.ones_like(wide), jnp.zeros_like(wide)
    for k in range(1, ANGLES):
        here = jnp.abs(wide - k) < 0.5
        cosine = jnp.where(here, math.cos(math.pi / ANGLES * k), cosine)
        sine = jnp.where(here, math.sin(math.pi / ANGLES * k), sine)
    return cosine * cosine, sine * sine, cosine * sine


def law(e, lam, mu2, stiff, angle):
    cc, ss, cs = angle
    trace = lam * (e[0] + e[1] + e[2])
    normal = stiff * (cc * e[0] + ss * e[2] + 2.0 * cs * e[4])
    dyad = (cc, None, ss, None, cs, None)
    out = []
    for k in range(6):
        value = mu2 * e[k]
        if k < 3:
            value = value + trace
        if dyad[k] is not None:
            value = value + normal * dyad[k]
        out.append(value)
    return out


def far_first(sizes, hops):
    offsets = [o for o in itertools.product(*[range(n) for n in sizes]) if any(o)]
    return sorted(offsets, key=lambda o: -sum(h(v) for h, v in zip(hops, o)))


def ring(v):
    return min(v, 4 - v)


def kernel(
    moduli, mean, strain_hbm, labels_hbm, normals_hbm, left_hbm, right_hbm, fwd_hbm, inv_hbm, twz_hbm, twx_hbm,
    strain_out, stress_out,
    strain, labels, normals, left_ref, right_ref, fwd_ref, inv_ref, twz_ref, twx_ref,
    s1, r1, s2, r2, s3, r3, s4, r4,
    load, send, recv, ready,
):
    zs, xs = lax.axis_size("gz"), lax.axis_size("gx")
    total = zs * xs
    j = lax.axis_index("gz")
    i = lax.axis_index("gx")
    me = zs * i + j
    z, x, core = j // 2, i // 4, lax.rem(i, 2)
    y = 2 * lax.rem(j, 2) + lax.rem(i // 2, 2)

    def peer(dx, dy, dz, dc):
        px, py, pz, pc = lax.rem(x + dx, 4), lax.rem(y + dy, 4), lax.rem(z + dz, 4), lax.rem(core + dc, 2)
        return 2 * pz + py // 2, 4 * px + 2 * lax.rem(py, 2) + pc

    z_peers = [peer(0, dy, dz, 0) for dz, dy in far_first((4, 3), (ring, ring)) if dy != 1]
    everyone = far_first((4, 4, 4, 2), (ring, ring, ring, lambda v: 0))

    def x_index(dx, dy, dc):
        low = lax.rem(i // 2 + dy, 2)
        return 4 * lax.rem(x + dx, 4) + 2 * low + lax.rem(core + dc, 2)

    x_peers = [x_index(*o) for o in far_first((4, 2, 2), (ring, lambda v: v, lambda v: 0))]

    barrier = pltpu.get_barrier_semaphore()
    for to, _ in z_peers:
        pl.semaphore_signal(barrier, inc=1, device_id={"gz": to, "gx": i}, device_id_type=MESH)
    for to in x_peers:
        pl.semaphore_signal(barrier, inc=1, device_id={"gz": j, "gx": to}, device_id_type=MESH)

    loads = [
        pltpu.make_async_copy(a, b, load.at[k])
        for k, (a, b) in enumerate((
            (strain_hbm, strain), (labels_hbm, labels), (normals_hbm, normals), (twz_hbm, twz_ref),
            (left_hbm, left_ref), (twx_hbm, twx_ref), (fwd_hbm, fwd_ref), (inv_hbm, inv_ref), (right_hbm, right_ref),
        ))
    ]
    for copy in loads:
        copy.start()
    for copy in loads[:3]:
        copy.wait()

    m = [moduli[k] for k in range(5)]
    lame_ref = 0.5 * (m[0] + m[2])
    shear_ref = 0.5 * (m[1] + m[3])
    for s in range(2):
        angle = orient(normals[s], s)
        lam, mu, stiff = stress_terms(m, labels[s])
        e = [strain[c, s] for c in range(6)]
        pol = law(e, lam - lame_ref, 2.0 * (mu - shear_ref), stiff, angle)
        for slot, c in enumerate(COMPS):
            for g in range(8):
                s1[g, 2 * slot + s] = pol[c][8 * g : 8 * g + 8, :]

    pl.semaphore_wait(barrier, zs + xs - 2)
    for to in x_peers:
        pl.semaphore_signal(ready, inc=1, device_id={"gz": j, "gx": to}, device_id_type=MESH)

    def z_exchange(src, dst, n):
        for to, _ in z_peers:
            pltpu.make_async_remote_copy(
                src_ref=src.at[to], dst_ref=dst.at[j], send_sem=send.at[n], recv_sem=recv.at[n],
                device_id={"gz": to, "gx": i}, device_id_type=MESH,
            ).start()
        dst[j] = src[j]
        pltpu.make_async_copy(dst.at[pl.ds(0, zs - 1)], dst.at[pl.ds(0, zs - 1)], recv.at[n]).wait()

    def all_exchange(src, dst, n):
        mine = pl.multiple_of(me * 8, 8)
        for o in everyone:
            tz, tx = peer(*o)
            there = pl.multiple_of((zs * tx + tz) * 8, 8)
            pltpu.make_async_remote_copy(
                src_ref=src.at[pl.ds(there, 5), :], dst_ref=dst.at[pl.ds(mine, 5), :],
                send_sem=send.at[n], recv_sem=recv.at[n],
                device_id={"gz": tz, "gx": tx}, device_id_type=MESH,
            ).start()
        dst[pl.ds(mine, 8), :] = src[pl.ds(mine, 8), :]
        rest = dst.at[pl.ds(0, 5 * (total - 1)), :]
        pltpu.make_async_copy(rest, rest, recv.at[n]).wait()

    def gathered(ref):
        return [ref[pl.ds(c, 128, stride=8), :] for c in range(5)]

    def scatter(ref, value):
        for c in range(5):
            ref[pl.ds(c, 128, stride=8), :] = value[:, 128 * c : 128 * c + 128]

    z_exchange(s1, r1, 0)
    for copy in loads[3:]:
        copy.wait()
    tabs = [ref[...] for ref in (left_ref, right_ref, fwd_ref, inv_ref, twz_ref, twx_ref)]
    twz = tabs[4]
    scatter(s2, mul(tabs[0], split3(z_forward(lambda a, b: r1[a, b], twz), 1), 1, 1))

    pl.semaphore_wait(ready, xs - 1)
    all_exchange(s2, r2, 1)
    scale = -1.0 / (1024.0 * 1024.0)
    half = scale * 0.5 / shear_ref
    couple = scale * (lame_ref + shear_ref) / (shear_ref * (lame_ref + 2.0 * shear_ref))
    scatter(s3, middle(jnp.concatenate(gathered(r2), axis=1), 8 * me, half, couple, tabs))

    all_exchange(s3, r3, 2)
    flat = jnp.concatenate([w.T for w in gathered(r3)], axis=0)
    parts = mul(split3(flat, 1), tabs[1])
    for c in range(5):
        tiles = z_inverse(parts[128 * c : 128 * c + 128], twz)
        for g in range(8):
            s4[g, 2 * c] = tiles[g][0]
            s4[g, 2 * c + 1] = tiles[g][1]

    z_exchange(s4, r4, 3)
    for s in range(2):
        angle = orient(normals[s], s)
        lam, mu, stiff = stress_terms(m, labels[s])
        e = [None] * 6
        for slot, c in enumerate(COMPS):
            e[c] = jnp.concatenate([r4[g, 2 * slot + s] for g in range(8)], axis=0) + mean[c]
        e[1] = jnp.full((64, 128), mean[1], jnp.float32)
        stress = law(e, lam, 2.0 * mu, stiff, angle)
        for c in range(6):
            strain_out[c, s] = e[c]
            stress_out[c, s] = stress[c]

    for n, ref in ((0, s1), (3, s4)):
        part = ref.at[pl.ds(0, zs - 1)]
        pltpu.make_async_copy(part, part, send.at[n]).wait()
    for n, ref in ((1, s2), (2, s3)):
        part = ref.at[pl.ds(0, 5 * (total - 1)), :]
        pltpu.make_async_copy(part, part, send.at[n]).wait()


def solution(mesh):
    consts = tables()

    def shards(strain, labels, normals, moduli, mean_strain):
        vmem = pl.BlockSpec(memory_space=pltpu.VMEM)
        smem = pl.BlockSpec(memory_space=pltpu.SMEM)
        away = pl.BlockSpec(memory_space=pl.ANY)
        arrays = [strain, labels, normals] + [jnp.asarray(a) for a in consts]
        tile = pltpu.VMEM((8, 10, 8, 128), jnp.float32)
        wide = pltpu.VMEM((1024, 128), jnp.float32)
        return tuple(
            pl.pallas_call(
                kernel,
                out_shape=[pltpu.VMEM(strain.shape, jnp.float32)] * 2,
                in_specs=[smem, smem] + [away] * len(arrays),
                out_specs=[vmem, vmem],
                scratch_shapes=[pltpu.VMEM(a.shape, a.dtype) for a in arrays]
                + [tile, tile, wide, wide, wide, wide, tile, tile]
                + [pltpu.SemaphoreType.DMA((len(arrays),)), pltpu.SemaphoreType.DMA((4,))]
                + [pltpu.SemaphoreType.DMA((4,)), pltpu.SemaphoreType.REGULAR],
                compiler_params=pltpu.CompilerParams(collective_id=0, has_side_effects=True),
            )(moduli, mean_strain, *arrays)
        )

    in_specs = (P(None, None, "gx", "gz"), P(None, "gx", "gz"), P(None, "gx", "gz"), P(), P())
    out_specs = (P(None, None, "gx", "gz"), P(None, None, "gx", "gz"))
    return jax.shard_map(shards, mesh=mesh, in_specs=in_specs, out_specs=out_specs, check_vma=False)
```

```python
import itertools
import math

import jax
import jax.numpy as jnp
import numpy as np
from jax import lax
from jax.experimental import pallas as pl
from jax.experimental.pallas import tpu as pltpu
from jax.sharding import PartitionSpec as P

ANGLES = 8
BLK = 16
COMPS = (0, 2, 4, 3, 5)
GROUPS = ((0, 3), (3, 2))
MESH = pl.DeviceIdType.MESH
HIGH = lax.Precision.HIGHEST
ROOT = math.sqrt(0.5)


def tables():
    k = np.arange(128)
    w = 2.0 * np.pi / 128.0 * (k[:, None] * k[None, :] % 128)
    dft = np.concatenate([np.cos(w), np.sin(w)], axis=1)
    r = np.arange(8)
    wz = 2.0 * np.pi / 1024.0 * (r[:, None] * k[None, :])
    twz = np.concatenate([np.cos(wz), np.sin(wz)], axis=0)
    lane = np.arange(128)
    t, low = lane // 64, lane % 8
    wx = 2.0 * np.pi / 1024.0 * (k[:, None] * low[None, :])
    sign = np.where(t == 0, 1.0, -1.0)[None, :]
    twx = np.concatenate([np.cos(wx), np.sin(wx) * sign], axis=0)
    same = (lane // 8 % 8)[:, None] == (lane // 8 % 8)[None, :]
    w8 = 2.0 * np.pi / 8.0 * (low[:, None] * low[None, :] % 8)
    ta, tb = t[:, None], t[None, :]
    cos8, sin8 = np.cos(w8) * same, np.sin(w8) * same
    fwd = np.where(ta == tb, cos8, np.where(ta == 1, sin8, -sin8))
    inv = np.where(ta == tb, cos8, np.where(ta == 1, -sin8, sin8))
    fwd2 = np.concatenate([fwd, np.roll(fwd, 64, axis=0)], axis=0)
    inv2 = np.concatenate([inv, np.roll(inv, 64, axis=1)], axis=1)
    twz, twx = np.asarray(twz, np.float32), np.asarray(twx, np.float32)
    return [left_table(dft), right_table(dft), right_table(fwd2), right_table(inv2), twz, twx]


def halves(a):
    a = np.asarray(a, np.float32)
    high = a.astype(jnp.bfloat16)
    return high, (a - high.astype(np.float32)).astype(jnp.bfloat16)


def left_table(a):
    high, low = halves(a)
    return np.concatenate([high, low, high], axis=1)


def right_table(a):
    high, low = halves(a)
    return np.concatenate([high, low, high], axis=0)


def split3(x, axis):
    high = x.astype(jnp.bfloat16)
    low = (x - high.astype(jnp.float32)).astype(jnp.bfloat16)
    return jnp.concatenate([high, high, low], axis=axis)


def mul(a, b, ca=1, cb=0):
    return lax.dot_general(a, b, (((ca,), (cb,)), ((), ())), preferred_element_type=jnp.float32)


def dot(a, b):
    return lax.dot_general(
        a, b, (((1,), (0,)), ((), ())), precision=HIGH, preferred_element_type=jnp.float32
    )


def fft8(u, sign):
    def add(a, b):
        return (a[0] + b[0], a[1] + b[1])

    def sub(a, b):
        return (a[0] - b[0], a[1] - b[1])

    def turn(a):
        return (-a[1], a[0]) if sign > 0 else (a[1], -a[0])

    def fft4(v):
        e, f = add(v[0], v[2]), sub(v[0], v[2])
        g, h = add(v[1], v[3]), turn(sub(v[1], v[3]))
        return [add(e, g), add(f, h), sub(e, g), sub(f, h)]

    even, odd = fft4(u[0::2]), fft4(u[1::2])
    o1, o3 = odd[1], odd[3]
    t1, t3 = turn(o1), turn(o3)
    odd = [
        odd[0],
        ((o1[0] + t1[0]) * ROOT, (o1[1] + t1[1]) * ROOT),
        turn(odd[2]),
        ((t3[0] - o3[0]) * ROOT, (t3[1] - o3[1]) * ROOT),
    ]
    return [add(even[k], odd[k]) for k in range(4)] + [sub(even[k], odd[k]) for k in range(4)]


def z_forward(load, twz, slots):
    blocks = []
    for c in slots:
        u = fft8([(load(j, 2 * c), load(j, 2 * c + 1)) for j in range(8)], -1)
        real, imag = [], []
        for r in range(8):
            re, im = u[r]
            if r:
                co, si = twz[r : r + 1, :], twz[8 + r : 9 + r, :]
                re, im = re * co + im * si, im * co - re * si
            real.append(re)
            imag.append(im)
        re, im = jnp.concatenate(real, axis=0), jnp.concatenate(imag, axis=0)
        left = jnp.concatenate([re, im], axis=0)
        right = jnp.concatenate([im, -re], axis=0)
        blocks.append(jnp.concatenate([left, right], axis=1))
    return jnp.concatenate(blocks, axis=0)


def z_inverse(parts, twz):
    v = []
    for r in range(8):
        lo, hi = slice(8 * r, 8 * r + 8), slice(64 + 8 * r, 72 + 8 * r)
        re = parts[lo, :128] - parts[hi, 128:]
        im = parts[hi, :128] + parts[lo, 128:]
        if r:
            co, si = twz[r : r + 1, :], twz[8 + r : 9 + r, :]
            re, im = re * co - im * si, im * co + re * si
        v.append((re, im))
    return fft8(v, 1)


def green_maps(kz_base):
    row = lax.broadcasted_iota(jnp.int32, (128, 128), 0)
    lane = lax.broadcasted_iota(jnp.int32, (128, 128), 1)
    kx = row + 128 * (lane % 8)
    kz = kz_base + lane // 8 % 8
    fx = jnp.where(kx < 512, kx, kx - 1024).astype(jnp.float32)
    fz = jnp.where(kz < 512, kz, kz - 1024).astype(jnp.float32)
    xx, zz, xz = fx * fx, fz * fz, fx * fz
    size = xx + zz
    inv = 1.0 / jnp.where(size == 0.0, 1.0, size)
    p, q, r = xx * inv, zz * inv, xz * inv
    return p, q, jnp.where((kx == 512) != (kz == 512), 0.0, r), p * q


def green(spec, maps, half, couple):
    p, q, r, pq = maps
    if len(spec) == 2:
        s3, s5 = spec
        return half * (s5 * r + s3 * q), half * (s5 * p + s3 * r)
    s0, s2, s4 = spec
    even, cross = s0 * p + s2 * q, s4 * r
    load = couple * (even + 2.0 * cross)
    return (
        2.0 * half * (s0 * p + cross) - load * p,
        2.0 * half * (s2 * q + cross) - load * q,
        half * (r * (s0 + s2) + s4 * (p + q)) - couple * (r * even + 2.0 * (s4 * pq)),
    )


def middle(wide, maps, half, couple, tabs):
    left, _, fwd, inv, _, twx = tabs
    n = wide.shape[1] // 128
    lane = lax.broadcasted_iota(jnp.int32, (128, 128), 1)
    sign = jnp.where(lane < 64, 1.0, -1.0)
    cx, sx = twx[:128, :], twx[128:, :]

    def lanes(x, c):
        return x[:, 128 * c : 128 * c + 128]

    def rows(x, c):
        return x[128 * c : 128 * c + 128]

    pairs = [jnp.concatenate([lanes(wide, c), swap(lanes(wide, c)) * sign], axis=0) for c in range(n)]
    x1 = mul(left, split3(jnp.concatenate(pairs, axis=1), 0))
    turned = [jnp.concatenate([lanes(x1, c) * cx, -(lanes(x1, c) * sx)], axis=1) for c in range(n)]
    spec = mul(split3(jnp.concatenate(turned, axis=0), 1), fwd)
    new = green([rows(spec, c) for c in range(n)], maps, half, couple)
    both = mul(split3(jnp.concatenate(new, axis=0), 1), inv)
    out = []
    for c in range(n):
        y, ry = rows(both, c)[:, :128], rows(both, c)[:, 128:]
        out.append(jnp.concatenate([y * cx - ry * sx, -((ry * cx + y * sx) * sign)], axis=0))
    return mul(left, split3(jnp.concatenate(out, axis=1), 0))


def swap(x):
    return pltpu.roll(x, 64, axis=1)


def stress_terms(moduli, labels):
    lam = jnp.where(labels == 1, moduli[2], moduli[0])
    mu = jnp.where(labels == 1, moduli[3], moduli[1])
    stiff = moduli[4] * labels.astype(jnp.float32)
    return lam, mu, stiff


def orient(normals, s):
    steps = normals.astype(jnp.float32)
    rows = lax.broadcasted_iota(jnp.int32, (64, 4), 0) // BLK == lax.broadcasted_iota(jnp.int32, (64, 4), 1)
    cols = lax.broadcasted_iota(jnp.int32, (8, 128), 0) == lax.broadcasted_iota(jnp.int32, (8, 128), 1) // BLK
    wide = dot(dot(rows.astype(jnp.float32), steps), cols.astype(jnp.float32))
    cosine, sine = jnp.ones_like(wide), jnp.zeros_like(wide)
    for k in range(1, ANGLES):
        here = jnp.abs(wide - k) < 0.5
        cosine = jnp.where(here, math.cos(math.pi / ANGLES * k), cosine)
        sine = jnp.where(here, math.sin(math.pi / ANGLES * k), sine)
    return cosine * cosine, sine * sine, cosine * sine


def law(e, lam, mu2, stiff, angle):
    cc, ss, cs = angle
    trace = lam * (e[0] + e[1] + e[2])
    normal = stiff * (cc * e[0] + ss * e[2] + 2.0 * cs * e[4])
    dyad = (cc, None, ss, None, cs, None)
    out = []
    for k in range(6):
        value = mu2 * e[k]
        if k < 3:
            value = value + trace
        if dyad[k] is not None:
            value = value + normal * dyad[k]
        out.append(value)
    return out


def far_first(sizes, hops):
    offsets = [o for o in itertools.product(*[range(n) for n in sizes]) if any(o)]
    return sorted(offsets, key=lambda o: -sum(h(v) for h, v in zip(hops, o)))


def ring(v):
    return min(v, 4 - v)


def kernel(
    moduli, mean, strain_hbm, labels_hbm, normals_hbm, left_hbm, right_hbm, fwd_hbm, inv_hbm, twz_hbm, twx_hbm,
    strain_out, stress_out,
    strain, labels, normals, left_ref, right_ref, fwd_ref, inv_ref, twz_ref, twx_ref,
    s1, r1, s2, r2, s3, r3, s4, r4, cells, maps,
    load, send, recv, ready,
):
    zs, xs = lax.axis_size("gz"), lax.axis_size("gx")
    total = zs * xs
    j = lax.axis_index("gz")
    i = lax.axis_index("gx")
    me = zs * i + j
    z, x, core = j // 2, i // 4, lax.rem(i, 2)
    y = 2 * lax.rem(j, 2) + lax.rem(i // 2, 2)

    px = [4 * lax.rem(x + d, 4) for d in range(4)]
    py = [lax.rem(y + d, 4) for d in range(4)]
    pz = [2 * lax.rem(z + d, 4) for d in range(4)]
    pc = [lax.rem(core + d, 2) for d in range(2)]
    high, low = [v // 2 for v in py], [2 * lax.rem(v, 2) for v in py]

    def peer(dx, dy, dz, dc):
        return pz[dz] + high[dy], px[dx] + low[dy] + pc[dc]

    z_peers = [peer(0, dy, dz, 0) for dz, dy in far_first((4, 3), (ring, ring)) if dy != 1]
    everyone = far_first((4, 4, 4, 2), (ring, ring, ring, lambda v: 0))

    def x_index(dx, dy, dc):
        low = lax.rem(i // 2 + dy, 2)
        return 4 * lax.rem(x + dx, 4) + 2 * low + lax.rem(core + dc, 2)

    x_peers = [x_index(*o) for o in far_first((4, 2, 2), (ring, lambda v: v, lambda v: 0))]

    barrier = pltpu.get_barrier_semaphore()
    for to, _ in z_peers:
        pl.semaphore_signal(barrier, inc=1, device_id={"gz": to, "gx": i}, device_id_type=MESH)
    for to in x_peers:
        pl.semaphore_signal(barrier, inc=1, device_id={"gz": j, "gx": to}, device_id_type=MESH)

    loads = [
        pltpu.make_async_copy(a, b, load.at[k])
        for k, (a, b) in enumerate((
            (strain_hbm, strain), (labels_hbm, labels), (normals_hbm, normals), (twz_hbm, twz_ref),
            (left_hbm, left_ref), (twx_hbm, twx_ref), (fwd_hbm, fwd_ref), (inv_hbm, inv_ref), (right_hbm, right_ref),
        ))
    ]
    for copy in loads:
        copy.start()
    for copy in loads[:3]:
        copy.wait()

    m = [moduli[k] for k in range(5)]
    lame_ref = 0.5 * (m[0] + m[2])
    shear_ref = 0.5 * (m[1] + m[3])
    for s in range(2):
        angle = orient(normals[s], s)
        lam, mu, stiff = stress_terms(m, labels[s])
        e = [strain[c, s] for c in range(6)]
        pol = law(e, lam - lame_ref, 2.0 * (mu - shear_ref), stiff, angle)
        for slot, c in enumerate(COMPS):
            for g in range(8):
                s1[g, 2 * slot + s] = pol[c][8 * g : 8 * g + 8, :]
        for k, value in enumerate((lam, 2.0 * mu, stiff, *angle)):
            cells[s, k] = value

    pl.semaphore_wait(barrier, zs + xs - 2)
    for to in x_peers:
        pl.semaphore_signal(ready, inc=1, device_id={"gz": j, "gx": to}, device_id_type=MESH)

    def z_send(src, dst, n, g):
        part = pl.ds(2 * GROUPS[g][0], 2 * GROUPS[g][1])
        for to, _ in z_peers:
            pltpu.make_async_remote_copy(
                src_ref=src.at[to, part], dst_ref=dst.at[j, part], send_sem=send.at[n, g], recv_sem=recv.at[n, g],
                device_id={"gz": to, "gx": i}, device_id_type=MESH,
            ).start()
        dst[j, part] = src[j, part]

    def z_wait(ref, sem, n, g):
        part = ref.at[pl.ds(0, zs - 1), pl.ds(2 * GROUPS[g][0], 2 * GROUPS[g][1])]
        pltpu.make_async_copy(part, part, sem.at[n, g]).wait()

    def all_send(src, dst, n, g):
        mine = pl.multiple_of(me * 8, 8)
        size = GROUPS[g][1]
        for o in everyone:
            tz, tx = peer(*o)
            there = pl.multiple_of((zs * tx + tz) * 8, 8)
            pltpu.make_async_remote_copy(
                src_ref=src.at[g, pl.ds(there, size), :], dst_ref=dst.at[g, pl.ds(mine, size), :],
                send_sem=send.at[n, g], recv_sem=recv.at[n, g],
                device_id={"gz": tz, "gx": tx}, device_id_type=MESH,
            ).start()
        dst[g, pl.ds(mine, 8), :] = src[g, pl.ds(mine, 8), :]

    def all_wait(ref, sem, n, g):
        part = ref.at[g, pl.ds(0, GROUPS[g][1] * (total - 1)), :]
        pltpu.make_async_copy(part, part, sem.at[n, g]).wait()

    def gathered(ref, g):
        return [ref[g, pl.ds(c, 128, stride=8), :] for c in range(GROUPS[g][1])]

    def scatter(ref, g, value):
        for c in range(GROUPS[g][1]):
            ref[g, pl.ds(c, 128, stride=8), :] = value[:, 128 * c : 128 * c + 128]

    for g in range(2):
        z_send(s1, r1, 0, g)
    scale = -1.0 / (1024.0 * 1024.0)
    half = scale * 0.5 / shear_ref
    couple = scale * (lame_ref + shear_ref) / (shear_ref * (lame_ref + 2.0 * shear_ref))
    for k, value in enumerate(green_maps(8 * me)):
        maps[k] = value
    for copy in loads[3:]:
        copy.wait()

    def table(ref):
        return ref[...]

    for g, (first, size) in enumerate(GROUPS):
        z_wait(r1, recv, 0, g)
        block = z_forward(lambda a, b: r1[a, b], table(twz_ref), range(first, first + size))
        scatter(s2, g, mul(table(left_ref), split3(block, 1), 1, 1))
        if g == 0:
            pl.semaphore_wait(ready, xs - 1)
        all_send(s2, r2, 1, g)

    for g in range(2):
        all_wait(r2, recv, 1, g)
        tabs = [table(ref) for ref in (left_ref, right_ref, fwd_ref, inv_ref, twz_ref, twx_ref)]
        wide = jnp.concatenate(gathered(r2, g), axis=1)
        scatter(s3, g, middle(wide, [maps[k] for k in range(4)], half, couple, tabs))
        all_send(s3, r3, 2, g)

    for g, (first, size) in enumerate(GROUPS):
        all_wait(r3, recv, 2, g)
        flat = jnp.concatenate([w.T for w in gathered(r3, g)], axis=0)
        parts = mul(split3(flat, 1), table(right_ref))
        for c in range(size):
            tiles = z_inverse(parts[128 * c : 128 * c + 128], table(twz_ref))
            for k in range(8):
                s4[k, 2 * (first + c)] = tiles[k][0]
                s4[k, 2 * (first + c) + 1] = tiles[k][1]
        z_send(s4, r4, 3, g)

    for g in range(2):
        z_wait(s1, send, 0, g)
        all_wait(s2, send, 1, g)
        all_wait(s3, send, 2, g)

    def arrived(slot, s):
        return jnp.concatenate([r4[k, 2 * slot + s] for k in range(8)], axis=0) + mean[COMPS[slot]]

    for g, (first, size) in enumerate(GROUPS):
        z_wait(r4, recv, 3, g)
        for s in range(2):
            e = [jnp.full((64, 128), mean[1], jnp.float32)] * 6
            for slot in range(first, first + size):
                e[COMPS[slot]] = arrived(slot, s)
            lam, mu2, stiff = (cells[s, k] for k in range(3))
            stress = law(e, lam, mu2, stiff, [cells[s, k] for k in range(3, 6)])
            done = [COMPS[k] for k in range(first, first + size)] + [1] * (g == 0)
            for c in done:
                strain_out[c, s] = e[c]
                stress_out[c, s] = stress[c]

    for g in range(2):
        z_wait(s4, send, 3, g)


def solution(mesh):
    consts = tables()

    def shards(strain, labels, normals, moduli, mean_strain):
        vmem = pl.BlockSpec(memory_space=pltpu.VMEM)
        smem = pl.BlockSpec(memory_space=pltpu.SMEM)
        away = pl.BlockSpec(memory_space=pl.ANY)
        arrays = [strain, labels, normals] + [jnp.asarray(a) for a in consts]
        tile = pltpu.VMEM((8, 10, 8, 128), jnp.float32)
        wide = pltpu.VMEM((2, 1024, 128), jnp.float32)
        return tuple(
            pl.pallas_call(
                kernel,
                out_shape=[pltpu.VMEM(strain.shape, jnp.float32)] * 2,
                in_specs=[smem, smem] + [away] * len(arrays),
                out_specs=[vmem, vmem],
                scratch_shapes=[pltpu.VMEM(a.shape, a.dtype) for a in arrays]
                + [tile, tile, wide, wide, wide, wide, tile, tile]
                + [pltpu.VMEM((2, 6, 64, 128), jnp.float32), pltpu.VMEM((4, 128, 128), jnp.float32)]
                + [pltpu.SemaphoreType.DMA((len(arrays),)), pltpu.SemaphoreType.DMA((4, 2))]
                + [pltpu.SemaphoreType.DMA((4, 2)), pltpu.SemaphoreType.REGULAR],
                compiler_params=pltpu.CompilerParams(collective_id=0, has_side_effects=True),
            )(moduli, mean_strain, *arrays)
        )

    in_specs = (P(None, None, "gx", "gz"), P(None, "gx", "gz"), P(None, "gx", "gz"), P(), P())
    out_specs = (P(None, None, "gx", "gz"), P(None, None, "gx", "gz"))
    return jax.shard_map(shards, mesh=mesh, in_specs=in_specs, out_specs=out_specs, check_vma=False)
```

```python
import itertools
import math

import jax
import jax.numpy as jnp
import numpy as np
from jax import lax
from jax.experimental import pallas as pl
from jax.experimental.pallas import tpu as pltpu
from jax.sharding import PartitionSpec as P

ANGLES = 8
BLK = 16
PARTS = 1
COMPS = (0, 2, 4, 3, 5)
GROUPS = ((0, 3), (3, 2))
MESH = pl.DeviceIdType.MESH
HIGH = lax.Precision.HIGHEST
ROOT = math.sqrt(0.5)


def tables():
    k = np.arange(128)
    w = 2.0 * np.pi / 128.0 * (k[:, None] * k[None, :] % 128)
    dft = np.concatenate([np.cos(w), np.sin(w)], axis=1)
    r = np.arange(8)
    wz = 2.0 * np.pi / 1024.0 * (r[:, None] * k[None, :])
    twz = np.concatenate([np.cos(wz), np.sin(wz)], axis=0)
    lane = np.arange(128)
    t, low = lane // 64, lane % 8
    wx = 2.0 * np.pi / 1024.0 * (k[:, None] * low[None, :])
    sign = np.where(t == 0, 1.0, -1.0)[None, :]
    twx = np.concatenate([np.cos(wx), np.sin(wx) * sign], axis=0)
    same = (lane // 8 % 8)[:, None] == (lane // 8 % 8)[None, :]
    w8 = 2.0 * np.pi / 8.0 * (low[:, None] * low[None, :] % 8)
    ta, tb = t[:, None], t[None, :]
    cos8, sin8 = np.cos(w8) * same, np.sin(w8) * same
    fwd = np.where(ta == tb, cos8, np.where(ta == 1, sin8, -sin8))
    inv = np.where(ta == tb, cos8, np.where(ta == 1, -sin8, sin8))
    fwd2 = np.concatenate([fwd, np.roll(fwd, 64, axis=0)], axis=0)
    inv2 = np.concatenate([inv, np.roll(inv, 64, axis=1)], axis=1)
    twz, twx = np.asarray(twz, np.float32), np.asarray(twx, np.float32)
    return [left_table(dft), right_table(dft), right_table(fwd2), right_table(inv2), twz, twx]


def halves(a):
    a = np.asarray(a, np.float32)
    high = a.astype(jnp.bfloat16)
    return high, (a - high.astype(np.float32)).astype(jnp.bfloat16)


def left_table(a):
    high, low = halves(a)
    return np.concatenate([high, low, high], axis=1)


def right_table(a):
    high, low = halves(a)
    return np.concatenate([high, low, high], axis=0)


def split3(x, axis):
    high = x.astype(jnp.bfloat16)
    low = (x - high.astype(jnp.float32)).astype(jnp.bfloat16)
    return jnp.concatenate([high, high, low], axis=axis)


def mul(a, b, ca=1, cb=0):
    return lax.dot_general(a, b, (((ca,), (cb,)), ((), ())), preferred_element_type=jnp.float32)


def dot(a, b):
    return lax.dot_general(
        a, b, (((1,), (0,)), ((), ())), precision=HIGH, preferred_element_type=jnp.float32
    )


def fft8(u, sign):
    def add(a, b):
        return (a[0] + b[0], a[1] + b[1])

    def sub(a, b):
        return (a[0] - b[0], a[1] - b[1])

    def turn(a):
        return (-a[1], a[0]) if sign > 0 else (a[1], -a[0])

    def fft4(v):
        e, f = add(v[0], v[2]), sub(v[0], v[2])
        g, h = add(v[1], v[3]), turn(sub(v[1], v[3]))
        return [add(e, g), add(f, h), sub(e, g), sub(f, h)]

    even, odd = fft4(u[0::2]), fft4(u[1::2])
    o1, o3 = odd[1], odd[3]
    t1, t3 = turn(o1), turn(o3)
    odd = [
        odd[0],
        ((o1[0] + t1[0]) * ROOT, (o1[1] + t1[1]) * ROOT),
        turn(odd[2]),
        ((t3[0] - o3[0]) * ROOT, (t3[1] - o3[1]) * ROOT),
    ]
    return [add(even[k], odd[k]) for k in range(4)] + [sub(even[k], odd[k]) for k in range(4)]


def z_forward(load, twz, slots):
    blocks = []
    for c in slots:
        u = fft8([(load(j, 2 * c), load(j, 2 * c + 1)) for j in range(8)], -1)
        real, imag = [], []
        for r in range(8):
            re, im = u[r]
            if r:
                co, si = twz[r : r + 1, :], twz[8 + r : 9 + r, :]
                re, im = re * co + im * si, im * co - re * si
            real.append(re)
            imag.append(im)
        re, im = jnp.concatenate(real, axis=0), jnp.concatenate(imag, axis=0)
        left = jnp.concatenate([re, im], axis=0)
        right = jnp.concatenate([im, -re], axis=0)
        blocks.append(jnp.concatenate([left, right], axis=1))
    return jnp.concatenate(blocks, axis=0)


def z_inverse(parts, twz):
    v = []
    for r in range(8):
        lo, hi = slice(8 * r, 8 * r + 8), slice(64 + 8 * r, 72 + 8 * r)
        re = parts[lo, :128] - parts[hi, 128:]
        im = parts[hi, :128] + parts[lo, 128:]
        if r:
            co, si = twz[r : r + 1, :], twz[8 + r : 9 + r, :]
            re, im = re * co - im * si, im * co + re * si
        v.append((re, im))
    return fft8(v, 1)


def green_maps(kz_base):
    row = lax.broadcasted_iota(jnp.int32, (128, 128), 0)
    lane = lax.broadcasted_iota(jnp.int32, (128, 128), 1)
    kx = row + 128 * (lane % 8)
    kz = kz_base + lane // 8 % 8
    fx = jnp.where(kx < 512, kx, kx - 1024).astype(jnp.float32)
    fz = jnp.where(kz < 512, kz, kz - 1024).astype(jnp.float32)
    xx, zz, xz = fx * fx, fz * fz, fx * fz
    size = xx + zz
    inv = 1.0 / jnp.where(size == 0.0, 1.0, size)
    p, q, r = xx * inv, zz * inv, xz * inv
    return p, q, jnp.where((kx == 512) != (kz == 512), 0.0, r), p * q


def green(spec, maps, half, couple):
    p, q, r, pq = maps
    if len(spec) == 2:
        s3, s5 = spec
        return half * (s5 * r + s3 * q), half * (s5 * p + s3 * r)
    s0, s2, s4 = spec
    even, cross = s0 * p + s2 * q, s4 * r
    load = couple * (even + 2.0 * cross)
    return (
        2.0 * half * (s0 * p + cross) - load * p,
        2.0 * half * (s2 * q + cross) - load * q,
        half * (r * (s0 + s2) + s4 * (p + q)) - couple * (r * even + 2.0 * (s4 * pq)),
    )


def middle(wide, maps, half, couple, tabs):
    left, _, fwd, inv, _, twx = tabs
    n = wide.shape[1] // 128
    lane = lax.broadcasted_iota(jnp.int32, (128, 128), 1)
    sign = jnp.where(lane < 64, 1.0, -1.0)
    cx, sx = twx[:128, :], twx[128:, :]

    def lanes(x, c):
        return x[:, 128 * c : 128 * c + 128]

    def rows(x, c):
        return x[128 * c : 128 * c + 128]

    pairs = [jnp.concatenate([lanes(wide, c), swap(lanes(wide, c)) * sign], axis=0) for c in range(n)]
    x1 = mul(left, split3(jnp.concatenate(pairs, axis=1), 0))
    turned = [jnp.concatenate([lanes(x1, c) * cx, -(lanes(x1, c) * sx)], axis=1) for c in range(n)]
    spec = mul(split3(jnp.concatenate(turned, axis=0), 1), fwd)
    new = green([rows(spec, c) for c in range(n)], maps, half, couple)
    both = mul(split3(jnp.concatenate(new, axis=0), 1), inv)
    out = []
    for c in range(n):
        y, ry = rows(both, c)[:, :128], rows(both, c)[:, 128:]
        out.append(jnp.concatenate([y * cx - ry * sx, -((ry * cx + y * sx) * sign)], axis=0))
    return mul(left, split3(jnp.concatenate(out, axis=1), 0))


def swap(x):
    return pltpu.roll(x, 64, axis=1)


def stress_terms(moduli, labels):
    lam = jnp.where(labels == 1, moduli[2], moduli[0])
    mu = jnp.where(labels == 1, moduli[3], moduli[1])
    stiff = moduli[4] * labels.astype(jnp.float32)
    return lam, mu, stiff


def orient(normals, s):
    steps = normals.astype(jnp.float32)
    rows = lax.broadcasted_iota(jnp.int32, (64, 4), 0) // BLK == lax.broadcasted_iota(jnp.int32, (64, 4), 1)
    cols = lax.broadcasted_iota(jnp.int32, (8, 128), 0) == lax.broadcasted_iota(jnp.int32, (8, 128), 1) // BLK
    wide = dot(dot(rows.astype(jnp.float32), steps), cols.astype(jnp.float32))
    cosine, sine = jnp.ones_like(wide), jnp.zeros_like(wide)
    for k in range(1, ANGLES):
        here = jnp.abs(wide - k) < 0.5
        cosine = jnp.where(here, math.cos(math.pi / ANGLES * k), cosine)
        sine = jnp.where(here, math.sin(math.pi / ANGLES * k), sine)
    return cosine * cosine, sine * sine, cosine * sine


def law(e, lam, mu2, stiff, angle):
    cc, ss, cs = angle
    trace = lam * (e[0] + e[1] + e[2])
    normal = stiff * (cc * e[0] + ss * e[2] + 2.0 * cs * e[4])
    dyad = (cc, None, ss, None, cs, None)
    out = []
    for k in range(6):
        value = mu2 * e[k]
        if k < 3:
            value = value + trace
        if dyad[k] is not None:
            value = value + normal * dyad[k]
        out.append(value)
    return out


def far_first(sizes, hops):
    offsets = [o for o in itertools.product(*[range(n) for n in sizes]) if any(o)]
    return sorted(offsets, key=lambda o: -sum(h(v) for h, v in zip(hops, o)))


def ring(v):
    return min(v, 4 - v)


def kernel(
    moduli, mean, strain_hbm, labels_hbm, normals_hbm, left_hbm, right_hbm, fwd_hbm, inv_hbm, twz_hbm, twx_hbm,
    strain_out, stress_out,
    strain, labels, normals, left_ref, right_ref, fwd_ref, inv_ref, twz_ref, twx_ref,
    *rest,
):
    s1, r1, s2, r2, s3, r3, s4, r4 = (rest[2 * k : 2 * k + 2] for k in range(8))
    cells, maps, load, send, recv, ready = rest[16:]
    zs, xs = lax.axis_size("gz"), lax.axis_size("gx")
    total = zs * xs
    j = lax.axis_index("gz")
    i = lax.axis_index("gx")
    me = zs * i + j
    z, x, core = j // 2, i // 4, lax.rem(i, 2)
    y = 2 * lax.rem(j, 2) + lax.rem(i // 2, 2)

    px = [4 * lax.rem(x + d, 4) for d in range(4)]
    py = [lax.rem(y + d, 4) for d in range(4)]
    pz = [2 * lax.rem(z + d, 4) for d in range(4)]
    pc = [lax.rem(core + d, 2) for d in range(2)]
    high, low = [v // 2 for v in py], [2 * lax.rem(v, 2) for v in py]

    def peer(dx, dy, dz, dc):
        return pz[dz] + high[dy], px[dx] + low[dy] + pc[dc]

    z_peers = [peer(0, dy, dz, 0) for dz, dy in far_first((4, 3), (ring, ring)) if dy != 1]
    early_first = [k + (k - j + zs) // zs for k in range(zs - 1)]
    everyone = far_first((4, 4, 4, 2), (ring, ring, ring, lambda v: 0))

    row = 2 * x + lax.rem(y, 2)
    early_rows = []
    for k, (rx, ry) in enumerate(sorted(itertools.product(range(4), range(2)), key=sum)):
        for dz, dy, dc in far_first((4, 2, 2), (ring, lambda v: 2 * v, lambda v: 0)):
            early_rows.append((pz[dz] + lax.rem(y // 2 + dy, 2), 4 * rx + 2 * ry + pc[dc]))
        if k < 7:
            other = k + (k - row + 8) // 8
            early_rows.append((j, 2 * other + core))

    def x_index(dx, dy, dc):
        low = lax.rem(i // 2 + dy, 2)
        return 4 * lax.rem(x + dx, 4) + 2 * low + lax.rem(core + dc, 2)

    x_peers = [x_index(*o) for o in far_first((4, 2, 2), (ring, lambda v: v, lambda v: 0))]

    barrier = pltpu.get_barrier_semaphore()
    for to, _ in z_peers:
        pl.semaphore_signal(barrier, inc=1, device_id={"gz": to, "gx": i}, device_id_type=MESH)
    for to in x_peers:
        pl.semaphore_signal(barrier, inc=1, device_id={"gz": j, "gx": to}, device_id_type=MESH)

    loads = [
        pltpu.make_async_copy(a, b, load.at[k])
        for k, (a, b) in enumerate((
            (strain_hbm, strain), (labels_hbm, labels), (normals_hbm, normals), (twz_hbm, twz_ref),
            (left_hbm, left_ref), (twx_hbm, twx_ref), (fwd_hbm, fwd_ref), (inv_hbm, inv_ref), (right_hbm, right_ref),
        ))
    ]
    for copy in loads:
        copy.start()
    for copy in loads[:3]:
        copy.wait()

    m = [moduli[k] for k in range(5)]
    lame_ref = 0.5 * (m[0] + m[2])
    shear_ref = 0.5 * (m[1] + m[3])
    for s in range(2):
        angle = orient(normals[s], s)
        lam, mu, stiff = stress_terms(m, labels[s])
        e = [strain[c, s] for c in range(6)]
        pol = law(e, lam - lame_ref, 2.0 * (mu - shear_ref), stiff, angle)
        for slot, c in enumerate(COMPS):
            for g in range(8):
                s1[slot // 3][g, 2 * (slot % 3) + s] = pol[c][8 * g : 8 * g + 8, :]
        for k, value in enumerate((lam, 2.0 * mu, stiff, *angle)):
            cells[s, k] = value

    pl.semaphore_wait(barrier, zs + xs - 2)
    for to in x_peers:
        pl.semaphore_signal(ready, inc=1, device_id={"gz": j, "gx": to}, device_id_type=MESH)

    def z_send(src, dst, n, g, peers):
        for to in peers:
            pltpu.make_async_remote_copy(
                src_ref=src[g].at[to], dst_ref=dst[g].at[j], send_sem=send.at[n, g], recv_sem=recv.at[n, g],
                device_id={"gz": to, "gx": i}, device_id_type=MESH,
            ).start()
        dst[g][j] = src[g][j]

    def z_wait(ref, sem, n, g):
        part = ref[g].at[pl.ds(0, zs - 1)]
        pltpu.make_async_copy(part, part, sem.at[n, g]).wait()

    def all_send(src, dst, n, g, peers):
        mine = pl.multiple_of(me * 8, 8)
        size = GROUPS[g][1]
        for tz, tx in peers:
            there = pl.multiple_of((zs * tx + tz) * 8, 8)
            pltpu.make_async_remote_copy(
                src_ref=src[g].at[pl.ds(there, size), :], dst_ref=dst[g].at[pl.ds(mine, size), :],
                send_sem=send.at[n, g], recv_sem=recv.at[n, g],
                device_id={"gz": tz, "gx": tx}, device_id_type=MESH,
            ).start()
        dst[g][pl.ds(mine, 8), :] = src[g][pl.ds(mine, 8), :]

    def all_wait(ref, sem, n, g):
        part = ref[g].at[pl.ds(0, GROUPS[g][1] * (total - 1)), :]
        pltpu.make_async_copy(part, part, sem.at[n, g]).wait()

    def gathered(ref, g):
        return [ref[g][pl.ds(c, 128, stride=8), :] for c in range(GROUPS[g][1])]

    def scatter(ref, g, value):
        for c in range(GROUPS[g][1]):
            ref[g][pl.ds(c, 128, stride=8), :] = value[:, 128 * c : 128 * c + 128]

    for g in range(2):
        z_send(s1, r1, 0, g, [to for to, _ in z_peers])
    scale = -1.0 / (1024.0 * 1024.0)
    half = scale * 0.5 / shear_ref
    couple = scale * (lame_ref + shear_ref) / (shear_ref * (lame_ref + 2.0 * shear_ref))
    for k, value in enumerate(green_maps(8 * me)):
        maps[k] = value
    for copy in loads[3:]:
        copy.wait()

    def table(ref):
        return ref[...]

    def forward(g):
        block = z_forward(lambda a, b: r1[g][a, b], table(twz_ref), range(GROUPS[g][1]))
        scatter(s2, g, mul(table(left_ref), split3(block, 1), 1, 1))

    def across(g):
        tabs = [table(ref) for ref in (left_ref, right_ref, fwd_ref, inv_ref, twz_ref, twx_ref)]
        wide = jnp.concatenate(gathered(r2, g), axis=1)
        scatter(s3, g, middle(wide, [maps[k] for k in range(4)], half, couple, tabs))

    def backward(g):
        flat = jnp.concatenate([w.T for w in gathered(r3, g)], axis=0)
        parts = mul(split3(flat, 1), table(right_ref))
        for c in range(GROUPS[g][1]):
            tiles = z_inverse(parts[128 * c : 128 * c + 128], table(twz_ref))
            for k in range(8):
                s4[g][k, 2 * c] = tiles[k][0]
                s4[g][k, 2 * c + 1] = tiles[k][1]

    for g in range(2):
        z_wait(r1, recv, 0, g)
        forward(g)
        if g == 0:
            pl.semaphore_wait(ready, xs - 1)
        all_send(s2, r2, 1, g, [peer(*o) for o in everyone])
    for g in range(2):
        all_wait(r2, recv, 1, g)
        across(g)
        all_send(s3, r3, 2, g, early_rows)
    for g in range(2):
        all_wait(r3, recv, 2, g)
        backward(g)
        z_send(s4, r4, 3, g, early_first)

    for g in range(2):
        z_wait(s1, send, 0, g)
        all_wait(s2, send, 1, g)
        all_wait(s3, send, 2, g)

    def arrived(slot, s):
        return jnp.concatenate([r4[slot // 3][k, 2 * (slot % 3) + s] for k in range(8)], axis=0) + mean[COMPS[slot]]

    for g, (first, size) in enumerate(GROUPS):
        z_wait(r4, recv, 3, g)
        for s in range(2):
            e = [jnp.full((64, 128), mean[1], jnp.float32)] * 6
            for slot in range(first, first + size):
                e[COMPS[slot]] = arrived(slot, s)
            lam, mu2, stiff = (cells[s, k] for k in range(3))
            stress = law(e, lam, mu2, stiff, [cells[s, k] for k in range(3, 6)])
            done = [COMPS[k] for k in range(first, first + size)] + [1] * (g == 0)
            for c in done:
                strain_out[c, s] = e[c]
                stress_out[c, s] = stress[c]

    for g in range(2):
        z_wait(s4, send, 3, g)


def put_out(strain, stress, strain_hbm, stress_hbm, sem):
    copies = []
    size = 6 // PARTS
    for k in range(PARTS):
        part = pl.ds(size * k, size)
        for n, (src, dst) in enumerate(((strain, strain_hbm), (stress, stress_hbm))):
            copies.append(pltpu.make_async_copy(src.at[part], dst.at[part], sem.at[n, k]))
    for copy in copies:
        copy.start()
    for copy in copies:
        copy.wait()


def solution(mesh):
    consts = tables()

    def shards(strain, labels, normals, moduli, mean_strain):
        vmem = pl.BlockSpec(memory_space=pltpu.VMEM)
        smem = pl.BlockSpec(memory_space=pltpu.SMEM)
        away = pl.BlockSpec(memory_space=pl.ANY)
        arrays = [strain, labels, normals] + [jnp.asarray(a) for a in consts]
        tiles = [pltpu.VMEM((8, 2 * n, 8, 128), jnp.float32) for _, n in GROUPS]
        wide = [pltpu.VMEM((1024, 128), jnp.float32)] * 2
        fields = pl.pallas_call(
            kernel,
            out_shape=[pltpu.VMEM(strain.shape, jnp.float32)] * 2,
            in_specs=[smem, smem] + [away] * len(arrays),
            out_specs=[vmem, vmem],
            scratch_shapes=[pltpu.VMEM(a.shape, a.dtype) for a in arrays]
            + tiles * 2 + wide * 4 + tiles * 2
            + [pltpu.VMEM((2, 6, 64, 128), jnp.float32), pltpu.VMEM((4, 128, 128), jnp.float32)]
            + [pltpu.SemaphoreType.DMA((len(arrays),)), pltpu.SemaphoreType.DMA((4, 2))]
            + [pltpu.SemaphoreType.DMA((4, 2)), pltpu.SemaphoreType.REGULAR],
            compiler_params=pltpu.CompilerParams(collective_id=0, has_side_effects=True),
        )(moduli, mean_strain, *arrays)
        return tuple(
            pl.pallas_call(
                put_out,
                out_shape=[jax.ShapeDtypeStruct(strain.shape, jnp.float32)] * 2,
                in_specs=[vmem] * 2,
                out_specs=[away] * 2,
                scratch_shapes=[pltpu.SemaphoreType.DMA((2, PARTS))],
            )(*[pltpu.with_memory_space_constraint(a, pltpu.VMEM) for a in fields])
        )

    in_specs = (P(None, None, "gx", "gz"), P(None, "gx", "gz"), P(None, "gx", "gz"), P(), P())
    out_specs = (P(None, None, "gx", "gz"), P(None, None, "gx", "gz"))
    return jax.shard_map(shards, mesh=mesh, in_specs=in_specs, out_specs=out_specs, check_vma=False)
```

```python
import itertools
import math

import jax
import jax.numpy as jnp
import numpy as np
from jax import lax
from jax.experimental import pallas as pl
from jax.experimental.pallas import tpu as pltpu
from jax.sharding import PartitionSpec as P

ANGLES = 8
BLK = 16
PARTS = 1
COMPS = (0, 2, 4, 3, 5)
GROUPS = ((0, 3), (3, 2))
MESH = pl.DeviceIdType.MESH
HIGH = lax.Precision.HIGHEST
ROOT = math.sqrt(0.5)


def tables():
    k = np.arange(128)
    w = 2.0 * np.pi / 128.0 * (k[:, None] * k[None, :] % 128)
    dft = np.concatenate([np.cos(w), np.sin(w)], axis=1)
    r = np.arange(8)
    wz = 2.0 * np.pi / 1024.0 * (r[:, None] * k[None, :])
    twz = np.concatenate([np.cos(wz), np.sin(wz)], axis=0)
    lane = np.arange(128)
    t, low = lane // 64, lane % 8
    wx = 2.0 * np.pi / 1024.0 * (k[:, None] * low[None, :])
    sign = np.where(t == 0, 1.0, -1.0)[None, :]
    twx = np.concatenate([np.cos(wx), np.sin(wx) * sign], axis=0)
    same = (lane // 8 % 8)[:, None] == (lane // 8 % 8)[None, :]
    w8 = 2.0 * np.pi / 8.0 * (low[:, None] * low[None, :] % 8)
    ta, tb = t[:, None], t[None, :]
    cos8, sin8 = np.cos(w8) * same, np.sin(w8) * same
    fwd = np.where(ta == tb, cos8, np.where(ta == 1, sin8, -sin8))
    inv = np.where(ta == tb, cos8, np.where(ta == 1, -sin8, sin8))
    fwd2 = np.concatenate([fwd, np.roll(fwd, 64, axis=0)], axis=0)
    inv2 = np.concatenate([inv, np.roll(inv, 64, axis=1)], axis=1)
    twz, twx = np.asarray(twz, np.float32), np.asarray(twx, np.float32)
    return [left_table(dft), right_table(dft), right_table(fwd2), right_table(inv2), twz, twx]


def halves(a):
    a = np.asarray(a, np.float32)
    high = a.astype(jnp.bfloat16)
    return high, (a - high.astype(np.float32)).astype(jnp.bfloat16)


def left_table(a):
    high, low = halves(a)
    return np.concatenate([high, low, high], axis=1)


def right_table(a):
    high, low = halves(a)
    return np.concatenate([high, low, high], axis=0)


def split3(x, axis):
    high = x.astype(jnp.bfloat16)
    low = (x - high.astype(jnp.float32)).astype(jnp.bfloat16)
    return jnp.concatenate([high, high, low], axis=axis)


def mul(a, b, ca=1, cb=0):
    return lax.dot_general(a, b, (((ca,), (cb,)), ((), ())), preferred_element_type=jnp.float32)


def dot(a, b):
    return lax.dot_general(
        a, b, (((1,), (0,)), ((), ())), precision=HIGH, preferred_element_type=jnp.float32
    )


def fft8(u, sign):
    def add(a, b):
        return (a[0] + b[0], a[1] + b[1])

    def sub(a, b):
        return (a[0] - b[0], a[1] - b[1])

    def turn(a):
        return (-a[1], a[0]) if sign > 0 else (a[1], -a[0])

    def fft4(v):
        e, f = add(v[0], v[2]), sub(v[0], v[2])
        g, h = add(v[1], v[3]), turn(sub(v[1], v[3]))
        return [add(e, g), add(f, h), sub(e, g), sub(f, h)]

    even, odd = fft4(u[0::2]), fft4(u[1::2])
    o1, o3 = odd[1], odd[3]
    t1, t3 = turn(o1), turn(o3)
    odd = [
        odd[0],
        ((o1[0] + t1[0]) * ROOT, (o1[1] + t1[1]) * ROOT),
        turn(odd[2]),
        ((t3[0] - o3[0]) * ROOT, (t3[1] - o3[1]) * ROOT),
    ]
    return [add(even[k], odd[k]) for k in range(4)] + [sub(even[k], odd[k]) for k in range(4)]


def z_forward(load, twz, slots):
    blocks = []
    for c in slots:
        u = fft8([(load(j, 2 * c), load(j, 2 * c + 1)) for j in range(8)], -1)
        real, imag = [], []
        for r in range(8):
            re, im = u[r]
            if r:
                co, si = twz[r : r + 1, :], twz[8 + r : 9 + r, :]
                re, im = re * co + im * si, im * co - re * si
            real.append(re)
            imag.append(im)
        re, im = jnp.concatenate(real, axis=0), jnp.concatenate(imag, axis=0)
        left = jnp.concatenate([re, im], axis=0)
        right = jnp.concatenate([im, -re], axis=0)
        blocks.append(jnp.concatenate([left, right], axis=1))
    return jnp.concatenate(blocks, axis=0)


def z_inverse(parts, twz):
    v = []
    for r in range(8):
        lo, hi = slice(8 * r, 8 * r + 8), slice(64 + 8 * r, 72 + 8 * r)
        re = parts[lo, :128] - parts[hi, 128:]
        im = parts[hi, :128] + parts[lo, 128:]
        if r:
            co, si = twz[r : r + 1, :], twz[8 + r : 9 + r, :]
            re, im = re * co - im * si, im * co + re * si
        v.append((re, im))
    return fft8(v, 1)


def green_maps(kz_base):
    row = lax.broadcasted_iota(jnp.int32, (128, 128), 0)
    lane = lax.broadcasted_iota(jnp.int32, (128, 128), 1)
    kx = row + 128 * (lane % 8)
    kz = kz_base + lane // 8 % 8
    fx = jnp.where(kx < 512, kx, kx - 1024).astype(jnp.float32)
    fz = jnp.where(kz < 512, kz, kz - 1024).astype(jnp.float32)
    xx, zz, xz = fx * fx, fz * fz, fx * fz
    size = xx + zz
    inv = 1.0 / jnp.where(size == 0.0, 1.0, size)
    p, q, r = xx * inv, zz * inv, xz * inv
    return p, q, jnp.where((kx == 512) != (kz == 512), 0.0, r), p * q


def green(spec, maps, half, couple):
    p, q, r, pq = maps
    if len(spec) == 2:
        s3, s5 = spec
        return half * (s5 * r + s3 * q), half * (s5 * p + s3 * r)
    s0, s2, s4 = spec
    even, cross = s0 * p + s2 * q, s4 * r
    load = couple * (even + 2.0 * cross)
    return (
        2.0 * half * (s0 * p + cross) - load * p,
        2.0 * half * (s2 * q + cross) - load * q,
        half * (r * (s0 + s2) + s4 * (p + q)) - couple * (r * even + 2.0 * (s4 * pq)),
    )


def middle(wide, maps, half, couple, tabs):
    left, _, fwd, inv, _, twx = tabs
    n = wide.shape[1] // 128
    lane = lax.broadcasted_iota(jnp.int32, (128, 128), 1)
    sign = jnp.where(lane < 64, 1.0, -1.0)
    cx, sx = twx[:128, :], twx[128:, :]

    def lanes(x, c):
        return x[:, 128 * c : 128 * c + 128]

    def rows(x, c):
        return x[128 * c : 128 * c + 128]

    pairs = [jnp.concatenate([lanes(wide, c), swap(lanes(wide, c)) * sign], axis=0) for c in range(n)]
    x1 = mul(left, split3(jnp.concatenate(pairs, axis=1), 0))
    turned = [jnp.concatenate([lanes(x1, c) * cx, -(lanes(x1, c) * sx)], axis=1) for c in range(n)]
    spec = mul(split3(jnp.concatenate(turned, axis=0), 1), fwd)
    new = green([rows(spec, c) for c in range(n)], maps, half, couple)
    both = mul(split3(jnp.concatenate(new, axis=0), 1), inv)
    out = []
    for c in range(n):
        y, ry = rows(both, c)[:, :128], rows(both, c)[:, 128:]
        out.append(jnp.concatenate([y * cx - ry * sx, -((ry * cx + y * sx) * sign)], axis=0))
    return mul(left, split3(jnp.concatenate(out, axis=1), 0))


def swap(x):
    return pltpu.roll(x, 64, axis=1)


def stress_terms(moduli, labels):
    lam = jnp.where(labels == 1, moduli[2], moduli[0])
    mu = jnp.where(labels == 1, moduli[3], moduli[1])
    stiff = moduli[4] * labels.astype(jnp.float32)
    return lam, mu, stiff


def orient(normals, s):
    steps = normals.astype(jnp.float32)
    rows = lax.broadcasted_iota(jnp.int32, (64, 4), 0) // BLK == lax.broadcasted_iota(jnp.int32, (64, 4), 1)
    cols = lax.broadcasted_iota(jnp.int32, (8, 128), 0) == lax.broadcasted_iota(jnp.int32, (8, 128), 1) // BLK
    wide = dot(dot(rows.astype(jnp.float32), steps), cols.astype(jnp.float32))
    cosine, sine = jnp.ones_like(wide), jnp.zeros_like(wide)
    for k in range(1, ANGLES):
        here = jnp.abs(wide - k) < 0.5
        cosine = jnp.where(here, math.cos(math.pi / ANGLES * k), cosine)
        sine = jnp.where(here, math.sin(math.pi / ANGLES * k), sine)
    return cosine * cosine, sine * sine, cosine * sine


def law(e, lam, mu2, stiff, angle):
    cc, ss, cs = angle
    trace = lam * (e[0] + e[1] + e[2])
    normal = stiff * (cc * e[0] + ss * e[2] + 2.0 * cs * e[4])
    dyad = (cc, None, ss, None, cs, None)
    out = []
    for k in range(6):
        value = mu2 * e[k]
        if k < 3:
            value = value + trace
        if dyad[k] is not None:
            value = value + normal * dyad[k]
        out.append(value)
    return out


def far_first(sizes, hops):
    offsets = [o for o in itertools.product(*[range(n) for n in sizes]) if any(o)]
    return sorted(offsets, key=lambda o: -sum(h(v) for h, v in zip(hops, o)))


def ring(v):
    return min(v, 4 - v)


def kernel(
    strain_hbm, labels_hbm, normals_hbm, moduli_hbm, mean_hbm, left_hbm, right_hbm, fwd_hbm, inv_hbm, twz_hbm, twx_hbm,
    strain_out, stress_out,
    strain, labels, normals, moduli, mean, left_ref, right_ref, fwd_ref, inv_ref, twz_ref, twx_ref,
    *rest,
):
    s1, r1, s2, r2, s3, r3, s4, r4 = (rest[2 * k : 2 * k + 2] for k in range(8))
    cells, maps, load, send, recv, ready = rest[16:]
    zs, xs = lax.axis_size("gz"), lax.axis_size("gx")
    total = zs * xs
    j = lax.axis_index("gz")
    i = lax.axis_index("gx")
    barrier = pltpu.get_barrier_semaphore()
    for k in (5, 3, 4, 1, 7, 2, 6):
        pl.semaphore_signal(barrier, inc=1, device_id={"gz": lax.rem(j + k, zs), "gx": i}, device_id_type=MESH)
    for k in (10, 6, 8, 11, 9, 7, 5, 12, 4, 13, 3, 14, 2, 15, 1):
        pl.semaphore_signal(barrier, inc=1, device_id={"gz": j, "gx": lax.rem(i + k, xs)}, device_id_type=MESH)

    loads = [
        pltpu.make_async_copy(a, b, load.at[k])
        for k, (a, b) in enumerate((
            (strain_hbm, strain), (labels_hbm, labels), (normals_hbm, normals), (moduli_hbm, moduli),
            (mean_hbm, mean), (twz_hbm, twz_ref),
            (left_hbm, left_ref), (twx_hbm, twx_ref), (fwd_hbm, fwd_ref), (inv_hbm, inv_ref), (right_hbm, right_ref),
        ))
    ]
    for copy in loads:
        copy.start()
    me = zs * i + j
    z, x, core = j // 2, i // 4, lax.rem(i, 2)
    y = 2 * lax.rem(j, 2) + lax.rem(i // 2, 2)

    px = [4 * lax.rem(x + d, 4) for d in range(4)]
    py = [lax.rem(y + d, 4) for d in range(4)]
    pz = [2 * lax.rem(z + d, 4) for d in range(4)]
    pc = [lax.rem(core + d, 2) for d in range(2)]
    high, low = [v // 2 for v in py], [2 * lax.rem(v, 2) for v in py]

    def peer(dx, dy, dz, dc):
        return pz[dz] + high[dy], px[dx] + low[dy] + pc[dc]

    z_peers = [peer(0, dy, dz, 0) for dz, dy in far_first((4, 3), (ring, ring)) if dy != 1]
    early_first = [k + (k - j + zs) // zs for k in range(zs - 1)]
    everyone = far_first((4, 4, 4, 2), (ring, ring, ring, lambda v: 0))

    row = 2 * x + lax.rem(y, 2)
    early_rows = []
    for k, (rx, ry) in enumerate(sorted(itertools.product(range(4), range(2)), key=sum)):
        for dz, dy, dc in far_first((4, 2, 2), (ring, lambda v: 2 * v, lambda v: 0)):
            early_rows.append((pz[dz] + lax.rem(y // 2 + dy, 2), 4 * rx + 2 * ry + pc[dc]))
        if k < 7:
            other = k + (k - row + 8) // 8
            early_rows.append((j, 2 * other + core))

    def x_index(dx, dy, dc):
        low = lax.rem(i // 2 + dy, 2)
        return 4 * lax.rem(x + dx, 4) + 2 * low + lax.rem(core + dc, 2)

    x_peers = [x_index(*o) for o in far_first((4, 2, 2), (ring, lambda v: v, lambda v: 0))]

    for copy in loads[:5]:
        copy.wait()

    m = [moduli[k] for k in range(5)]
    lame_ref = 0.5 * (m[0] + m[2])
    shear_ref = 0.5 * (m[1] + m[3])
    for s in range(2):
        angle = orient(normals[s], s)
        lam, mu, stiff = stress_terms(m, labels[s])
        e = [strain[c, s] for c in range(6)]
        pol = law(e, lam - lame_ref, 2.0 * (mu - shear_ref), stiff, angle)
        for slot, c in enumerate(COMPS):
            for g in range(8):
                s1[slot // 3][g, 2 * (slot % 3) + s] = pol[c][8 * g : 8 * g + 8, :]
        for k, value in enumerate((lam, 2.0 * mu, stiff, *angle)):
            cells[s, k] = value

    pl.semaphore_wait(barrier, zs + xs - 2)
    for to in x_peers:
        pl.semaphore_signal(ready, inc=1, device_id={"gz": j, "gx": to}, device_id_type=MESH)

    def z_send(src, dst, n, g, peers):
        for to in peers:
            pltpu.make_async_remote_copy(
                src_ref=src[g].at[to], dst_ref=dst[g].at[j], send_sem=send.at[n, g], recv_sem=recv.at[n, g],
                device_id={"gz": to, "gx": i}, device_id_type=MESH,
            ).start()
        dst[g][j] = src[g][j]

    def z_wait(ref, sem, n, g):
        part = ref[g].at[pl.ds(0, zs - 1)]
        pltpu.make_async_copy(part, part, sem.at[n, g]).wait()

    def all_send(src, dst, n, g, peers):
        mine = pl.multiple_of(me * 8, 8)
        size = GROUPS[g][1]
        for tz, tx in peers:
            there = pl.multiple_of((zs * tx + tz) * 8, 8)
            pltpu.make_async_remote_copy(
                src_ref=src[g].at[pl.ds(there, size), :], dst_ref=dst[g].at[pl.ds(mine, size), :],
                send_sem=send.at[n, g], recv_sem=recv.at[n, g],
                device_id={"gz": tz, "gx": tx}, device_id_type=MESH,
            ).start()
        dst[g][pl.ds(mine, 8), :] = src[g][pl.ds(mine, 8), :]

    def all_wait(ref, sem, n, g):
        part = ref[g].at[pl.ds(0, GROUPS[g][1] * (total - 1)), :]
        pltpu.make_async_copy(part, part, sem.at[n, g]).wait()

    def gathered(ref, g):
        return [ref[g][pl.ds(c, 128, stride=8), :] for c in range(GROUPS[g][1])]

    def scatter(ref, g, value):
        for c in range(GROUPS[g][1]):
            ref[g][pl.ds(c, 128, stride=8), :] = value[:, 128 * c : 128 * c + 128]

    for g in range(2):
        z_send(s1, r1, 0, g, [to for to, _ in z_peers])
    scale = -1.0 / (1024.0 * 1024.0)
    half = scale * 0.5 / shear_ref
    couple = scale * (lame_ref + shear_ref) / (shear_ref * (lame_ref + 2.0 * shear_ref))
    for k, value in enumerate(green_maps(8 * me)):
        maps[k] = value
    for copy in loads[5:]:
        copy.wait()

    def table(ref):
        return ref[...]

    def forward(g):
        block = z_forward(lambda a, b: r1[g][a, b], table(twz_ref), range(GROUPS[g][1]))
        scatter(s2, g, mul(table(left_ref), split3(block, 1), 1, 1))

    def across(g):
        tabs = [table(ref) for ref in (left_ref, right_ref, fwd_ref, inv_ref, twz_ref, twx_ref)]
        wide = jnp.concatenate(gathered(r2, g), axis=1)
        scatter(s3, g, middle(wide, [maps[k] for k in range(4)], half, couple, tabs))

    def backward(g):
        flat = jnp.concatenate([w.T for w in gathered(r3, g)], axis=0)
        parts = mul(split3(flat, 1), table(right_ref))
        for c in range(GROUPS[g][1]):
            tiles = z_inverse(parts[128 * c : 128 * c + 128], table(twz_ref))
            for k in range(8):
                s4[g][k, 2 * c] = tiles[k][0]
                s4[g][k, 2 * c + 1] = tiles[k][1]

    for g in range(2):
        z_wait(r1, recv, 0, g)
        forward(g)
        if g == 0:
            pl.semaphore_wait(ready, xs - 1)
        all_send(s2, r2, 1, g, [peer(*o) for o in everyone])
    for g in range(2):
        all_wait(r2, recv, 1, g)
        across(g)
        all_send(s3, r3, 2, g, early_rows)
    for g in range(2):
        all_wait(r3, recv, 2, g)
        backward(g)
        z_send(s4, r4, 3, g, early_first)

    for g in range(2):
        z_wait(s1, send, 0, g)
        all_wait(s2, send, 1, g)
        all_wait(s3, send, 2, g)

    def arrived(slot, s):
        return jnp.concatenate([r4[slot // 3][k, 2 * (slot % 3) + s] for k in range(8)], axis=0) + mean[COMPS[slot]]

    for g, (first, size) in enumerate(GROUPS):
        z_wait(r4, recv, 3, g)
        for s in range(2):
            e = [jnp.full((64, 128), mean[1], jnp.float32)] * 6
            for slot in range(first, first + size):
                e[COMPS[slot]] = arrived(slot, s)
            lam, mu2, stiff = (cells[s, k] for k in range(3))
            stress = law(e, lam, mu2, stiff, [cells[s, k] for k in range(3, 6)])
            done = [COMPS[k] for k in range(first, first + size)] + [1] * (g == 0)
            for c in done:
                strain_out[c, s] = e[c]
                stress_out[c, s] = stress[c]

    for g in range(2):
        z_wait(s4, send, 3, g)


def put_out(strain, stress, strain_hbm, stress_hbm, sem):
    copies = []
    size = 6 // PARTS
    for k in range(PARTS):
        part = pl.ds(size * k, size)
        for n, (src, dst) in enumerate(((strain, strain_hbm), (stress, stress_hbm))):
            copies.append(pltpu.make_async_copy(src.at[part], dst.at[part], sem.at[n, k]))
    for copy in copies:
        copy.start()
    for copy in copies:
        copy.wait()


def solution(mesh):
    consts = tables()

    def shards(strain, labels, normals, moduli, mean_strain):
        vmem = pl.BlockSpec(memory_space=pltpu.VMEM)
        away = pl.BlockSpec(memory_space=pl.ANY)
        arrays = [strain, labels, normals, moduli, mean_strain] + [jnp.asarray(a) for a in consts]
        tiles = [pltpu.VMEM((8, 2 * n, 8, 128), jnp.float32) for _, n in GROUPS]
        wide = [pltpu.VMEM((1024, 128), jnp.float32)] * 2
        fields = pl.pallas_call(
            kernel,
            out_shape=[pltpu.VMEM(strain.shape, jnp.float32)] * 2,
            in_specs=[away] * len(arrays),
            out_specs=[vmem, vmem],
            scratch_shapes=[(pltpu.SMEM if a.ndim == 1 else pltpu.VMEM)(a.shape, a.dtype) for a in arrays]
            + tiles * 2 + wide * 4 + tiles * 2
            + [pltpu.VMEM((2, 6, 64, 128), jnp.float32), pltpu.VMEM((4, 128, 128), jnp.float32)]
            + [pltpu.SemaphoreType.DMA((len(arrays),)), pltpu.SemaphoreType.DMA((4, 2))]
            + [pltpu.SemaphoreType.DMA((4, 2)), pltpu.SemaphoreType.REGULAR],
            compiler_params=pltpu.CompilerParams(collective_id=0, has_side_effects=True),
        )(*arrays)
        return tuple(
            pl.pallas_call(
                put_out,
                out_shape=[jax.ShapeDtypeStruct(strain.shape, jnp.float32)] * 2,
                in_specs=[vmem] * 2,
                out_specs=[away] * 2,
                scratch_shapes=[pltpu.SemaphoreType.DMA((2, PARTS))],
            )(*[pltpu.with_memory_space_constraint(a, pltpu.VMEM) for a in fields])
        )

    in_specs = (P(None, None, "gx", "gz"), P(None, "gx", "gz"), P(None, "gx", "gz"), P(), P())
    out_specs = (P(None, None, "gx", "gz"), P(None, None, "gx", "gz"))
    return jax.shard_map(shards, mesh=mesh, in_specs=in_specs, out_specs=out_specs, check_vma=False)
```

```python
import itertools
import math

import jax
import jax.numpy as jnp
import numpy as np
from jax import lax
from jax.experimental import pallas as pl
from jax.experimental.pallas import tpu as pltpu
from jax.sharding import PartitionSpec as P

ANGLES = 8
BLK = 16
PARTS = 1
COMPS = (0, 2, 4, 3, 5)
GROUPS = ((0, 3), (3, 2))
MESH = pl.DeviceIdType.MESH
HIGH = lax.Precision.HIGHEST
ROOT = math.sqrt(0.5)


def tables():
    k = np.arange(128)
    w = 2.0 * np.pi / 128.0 * (k[:, None] * k[None, :] % 128)
    dft = np.concatenate([np.cos(w), np.sin(w)], axis=1)
    r = np.arange(8)
    wz = 2.0 * np.pi / 1024.0 * (r[:, None] * k[None, :])
    twz = np.concatenate([np.cos(wz), np.sin(wz)], axis=0)
    lane = np.arange(128)
    t, low = lane // 64, lane % 8
    wx = 2.0 * np.pi / 1024.0 * (k[:, None] * low[None, :])
    sign = np.where(t == 0, 1.0, -1.0)[None, :]
    twx = np.concatenate([np.cos(wx), np.sin(wx) * sign], axis=0)
    same = (lane // 8 % 8)[:, None] == (lane // 8 % 8)[None, :]
    w8 = 2.0 * np.pi / 8.0 * (low[:, None] * low[None, :] % 8)
    ta, tb = t[:, None], t[None, :]
    cos8, sin8 = np.cos(w8) * same, np.sin(w8) * same
    fwd = np.where(ta == tb, cos8, np.where(ta == 1, sin8, -sin8))
    inv = np.where(ta == tb, cos8, np.where(ta == 1, -sin8, sin8))
    fwd2 = np.concatenate([fwd, np.roll(fwd, 64, axis=0)], axis=0)
    inv2 = np.concatenate([inv, np.roll(inv, 64, axis=1)], axis=1)
    twz, twx = np.asarray(twz, np.float32), np.asarray(twx, np.float32)
    stacked = np.concatenate([np.cos(w), np.sin(w)], axis=0)
    return [left_table(dft), right_table(dft), right_table(fwd2), right_table(inv2), twz, twx, left_table(stacked)]


def halves(a):
    a = np.asarray(a, np.float32)
    high = a.astype(jnp.bfloat16)
    return high, (a - high.astype(np.float32)).astype(jnp.bfloat16)


def left_table(a):
    high, low = halves(a)
    return np.concatenate([high, low, high], axis=1)


def right_table(a):
    high, low = halves(a)
    return np.concatenate([high, low, high], axis=0)


def split3(x, axis):
    high = x.astype(jnp.bfloat16)
    low = (x - high.astype(jnp.float32)).astype(jnp.bfloat16)
    return jnp.concatenate([high, high, low], axis=axis)


def mul(a, b, ca=1, cb=0):
    return lax.dot_general(a, b, (((ca,), (cb,)), ((), ())), preferred_element_type=jnp.float32)


def dot(a, b):
    return lax.dot_general(
        a, b, (((1,), (0,)), ((), ())), precision=HIGH, preferred_element_type=jnp.float32
    )


def fft8(u, sign):
    def add(a, b):
        return (a[0] + b[0], a[1] + b[1])

    def sub(a, b):
        return (a[0] - b[0], a[1] - b[1])

    def turn(a):
        return (-a[1], a[0]) if sign > 0 else (a[1], -a[0])

    def fft4(v):
        e, f = add(v[0], v[2]), sub(v[0], v[2])
        g, h = add(v[1], v[3]), turn(sub(v[1], v[3]))
        return [add(e, g), add(f, h), sub(e, g), sub(f, h)]

    even, odd = fft4(u[0::2]), fft4(u[1::2])
    o1, o3 = odd[1], odd[3]
    t1, t3 = turn(o1), turn(o3)
    odd = [
        odd[0],
        ((o1[0] + t1[0]) * ROOT, (o1[1] + t1[1]) * ROOT),
        turn(odd[2]),
        ((t3[0] - o3[0]) * ROOT, (t3[1] - o3[1]) * ROOT),
    ]
    return [add(even[k], odd[k]) for k in range(4)] + [sub(even[k], odd[k]) for k in range(4)]


def z_forward(load, twz, slots):
    blocks = []
    for c in slots:
        u = fft8([(load(j, 2 * c), load(j, 2 * c + 1)) for j in range(8)], -1)
        real, imag = [], []
        for r in range(8):
            re, im = u[r]
            if r:
                co, si = twz[r : r + 1, :], twz[8 + r : 9 + r, :]
                re, im = re * co + im * si, im * co - re * si
            real.append(re)
            imag.append(im)
        re, im = jnp.concatenate(real, axis=0), jnp.concatenate(imag, axis=0)
        left = jnp.concatenate([re, im], axis=0)
        right = jnp.concatenate([im, -re], axis=0)
        blocks.append(jnp.concatenate([left, right], axis=1))
    return jnp.concatenate(blocks, axis=0)


def z_inverse(parts, twz):
    v = []
    for r in range(8):
        lo, hi = slice(8 * r, 8 * r + 8), slice(64 + 8 * r, 72 + 8 * r)
        re = parts[lo, :128] - parts[hi, 128:]
        im = parts[hi, :128] + parts[lo, 128:]
        if r:
            co, si = twz[r : r + 1, :], twz[8 + r : 9 + r, :]
            re, im = re * co - im * si, im * co + re * si
        v.append((re, im))
    return fft8(v, 1)


def green_maps(kz_base):
    row = lax.broadcasted_iota(jnp.int32, (128, 128), 0)
    lane = lax.broadcasted_iota(jnp.int32, (128, 128), 1)
    kx = row + 128 * (lane % 8)
    kz = kz_base + lane // 8 % 8
    fx = jnp.where(kx < 512, kx, kx - 1024).astype(jnp.float32)
    fz = jnp.where(kz < 512, kz, kz - 1024).astype(jnp.float32)
    xx, zz, xz = fx * fx, fz * fz, fx * fz
    size = xx + zz
    inv = 1.0 / jnp.where(size == 0.0, 1.0, size)
    p, q, r = xx * inv, zz * inv, xz * inv
    return p, q, jnp.where((kx == 512) != (kz == 512), 0.0, r), p * q


def green(spec, maps, half, couple):
    p, q, r, pq = maps
    if len(spec) == 2:
        s3, s5 = spec
        return half * (s5 * r + s3 * q), half * (s5 * p + s3 * r)
    s0, s2, s4 = spec
    even, cross = s0 * p + s2 * q, s4 * r
    load = couple * (even + 2.0 * cross)
    return (
        2.0 * half * (s0 * p + cross) - load * p,
        2.0 * half * (s2 * q + cross) - load * q,
        half * (r * (s0 + s2) + s4 * (p + q)) - couple * (r * even + 2.0 * (s4 * pq)),
    )


def middle(wide, maps, half, couple, tabs):
    left, _, fwd, inv, _, twx, both_left = tabs
    n = wide.shape[1] // 128
    lane = lax.broadcasted_iota(jnp.int32, (128, 128), 1)
    sign = jnp.where(lane < 64, 1.0, -1.0)
    cx, sx = twx[:128, :], twx[128:, :]

    def lanes(x, c):
        return x[:, 128 * c : 128 * c + 128]

    def rows(x, c):
        return x[128 * c : 128 * c + 128]

    cs = mul(both_left, split3(wide, 0))
    turned = []
    for c in range(n):
        v, u = lanes(cs[:128], c), -(lanes(cs[128:], c) * sign)
        turned.append(jnp.concatenate([v * cx + u * sx, u * cx - v * sx], axis=1))
    spec = mul(split3(jnp.concatenate(turned, axis=0), 1), fwd)
    new = green([rows(spec, c) for c in range(n)], maps, half, couple)
    both = mul(split3(jnp.concatenate(new, axis=0), 1), inv)
    out = []
    for c in range(n):
        y, ry = rows(both, c)[:, :128], rows(both, c)[:, 128:]
        out.append(jnp.concatenate([y * cx - ry * sx, -((ry * cx + y * sx) * sign)], axis=0))
    return mul(left, split3(jnp.concatenate(out, axis=1), 0))


def stress_terms(moduli, labels):
    lam = jnp.where(labels == 1, moduli[2], moduli[0])
    mu = jnp.where(labels == 1, moduli[3], moduli[1])
    stiff = moduli[4] * labels.astype(jnp.float32)
    return lam, mu, stiff


def orient(normals, s):
    steps = normals.astype(jnp.float32)
    rows = lax.broadcasted_iota(jnp.int32, (64, 4), 0) // BLK == lax.broadcasted_iota(jnp.int32, (64, 4), 1)
    cols = lax.broadcasted_iota(jnp.int32, (8, 128), 0) == lax.broadcasted_iota(jnp.int32, (8, 128), 1) // BLK
    wide = dot(dot(rows.astype(jnp.float32), steps), cols.astype(jnp.float32))
    cosine, sine = jnp.ones_like(wide), jnp.zeros_like(wide)
    for k in range(1, ANGLES):
        here = jnp.abs(wide - k) < 0.5
        cosine = jnp.where(here, math.cos(math.pi / ANGLES * k), cosine)
        sine = jnp.where(here, math.sin(math.pi / ANGLES * k), sine)
    return cosine * cosine, sine * sine, cosine * sine


def law(e, lam, mu2, stiff, angle):
    cc, ss, cs = angle
    trace = lam * (e[0] + e[1] + e[2])
    normal = stiff * (cc * e[0] + ss * e[2] + 2.0 * cs * e[4])
    dyad = (cc, None, ss, None, cs, None)
    out = []
    for k in range(6):
        value = mu2 * e[k]
        if k < 3:
            value = value + trace
        if dyad[k] is not None:
            value = value + normal * dyad[k]
        out.append(value)
    return out


def far_first(sizes, hops):
    offsets = [o for o in itertools.product(*[range(n) for n in sizes]) if any(o)]
    return sorted(offsets, key=lambda o: -sum(h(v) for h, v in zip(hops, o)))


def ring(v):
    return min(v, 4 - v)


def kernel(
    strain_hbm, labels_hbm, normals_hbm, moduli_hbm, mean_hbm, left_hbm, right_hbm, fwd_hbm, inv_hbm, twz_hbm, twx_hbm, both_hbm,
    strain_out, stress_out,
    strain, labels, normals, moduli, mean, left_ref, right_ref, fwd_ref, inv_ref, twz_ref, twx_ref, both_ref,
    *rest,
):
    s1, r1, s2, r2, s3, r3, s4, r4 = (rest[2 * k : 2 * k + 2] for k in range(8))
    cells, maps, load, send, recv, ready = rest[16:]
    zs, xs = lax.axis_size("gz"), lax.axis_size("gx")
    total = zs * xs
    j = lax.axis_index("gz")
    i = lax.axis_index("gx")
    barrier = pltpu.get_barrier_semaphore()
    for k in (5, 3, 4, 1, 7, 2, 6):
        pl.semaphore_signal(barrier, inc=1, device_id={"gz": lax.rem(j + k, zs), "gx": i}, device_id_type=MESH)
    for k in (10, 6, 8, 11, 9, 7, 5, 12, 4, 13, 3, 14, 2, 15, 1):
        pl.semaphore_signal(barrier, inc=1, device_id={"gz": j, "gx": lax.rem(i + k, xs)}, device_id_type=MESH)

    loads = [
        pltpu.make_async_copy(a, b, load.at[k])
        for k, (a, b) in enumerate((
            (strain_hbm, strain), (labels_hbm, labels), (normals_hbm, normals), (moduli_hbm, moduli),
            (mean_hbm, mean), (twz_hbm, twz_ref),
            (left_hbm, left_ref), (twx_hbm, twx_ref), (fwd_hbm, fwd_ref), (inv_hbm, inv_ref), (right_hbm, right_ref),
            (both_hbm, both_ref),
        ))
    ]
    for copy in loads:
        copy.start()
    me = zs * i + j
    z, x, core = j // 2, i // 4, lax.rem(i, 2)
    y = 2 * lax.rem(j, 2) + lax.rem(i // 2, 2)

    px = [4 * lax.rem(x + d, 4) for d in range(4)]
    py = [lax.rem(y + d, 4) for d in range(4)]
    pz = [2 * lax.rem(z + d, 4) for d in range(4)]
    pc = [lax.rem(core + d, 2) for d in range(2)]
    high, low = [v // 2 for v in py], [2 * lax.rem(v, 2) for v in py]

    def peer(dx, dy, dz, dc):
        return pz[dz] + high[dy], px[dx] + low[dy] + pc[dc]

    z_peers = [peer(0, dy, dz, 0) for dz, dy in far_first((4, 3), (ring, ring)) if dy != 1]
    early_first = [k + (k - j + zs) // zs for k in range(zs - 1)]
    everyone = far_first((4, 4, 4, 2), (ring, ring, ring, lambda v: 0))

    row = 2 * x + lax.rem(y, 2)
    early_rows = []
    for k, (rx, ry) in enumerate(itertools.product(range(4), range(2))):
        for dz, dy, dc in far_first((4, 2, 2), (ring, lambda v: 2 * v, lambda v: 0)):
            early_rows.append((pz[dz] + lax.rem(y // 2 + dy, 2), 4 * rx + 2 * ry + pc[dc]))
        if k < 7:
            other = k + (k - row + 8) // 8
            early_rows.append((j, 2 * other + core))

    def x_index(dx, dy, dc):
        low = lax.rem(i // 2 + dy, 2)
        return 4 * lax.rem(x + dx, 4) + 2 * low + lax.rem(core + dc, 2)

    x_peers = [x_index(*o) for o in far_first((4, 2, 2), (ring, lambda v: v, lambda v: 0))]

    for copy in loads[:5]:
        copy.wait()

    m = [moduli[k] for k in range(5)]
    lame_ref = 0.5 * (m[0] + m[2])
    shear_ref = 0.5 * (m[1] + m[3])
    for s in range(2):
        angle = orient(normals[s], s)
        lam, mu, stiff = stress_terms(m, labels[s])
        e = [strain[c, s] for c in range(6)]
        pol = law(e, lam - lame_ref, 2.0 * (mu - shear_ref), stiff, angle)
        for slot, c in enumerate(COMPS):
            for g in range(8):
                s1[slot // 3][g, 2 * (slot % 3) + s] = pol[c][8 * g : 8 * g + 8, :]
        for k, value in enumerate((lam, 2.0 * mu, stiff, *angle)):
            cells[s, k] = value

    pl.semaphore_wait(barrier, zs + xs - 2)

    def z_send(src, dst, n, g, peers):
        for to in peers:
            pltpu.make_async_remote_copy(
                src_ref=src[g].at[to], dst_ref=dst[g].at[j], send_sem=send.at[n, g], recv_sem=recv.at[n, g],
                device_id={"gz": to, "gx": i}, device_id_type=MESH,
            ).start()

    def z_wait(ref, sem, n, g):
        part = ref[g].at[pl.ds(0, zs - 1)]
        pltpu.make_async_copy(part, part, sem.at[n, g]).wait()

    def all_send(src, dst, n, g, peers):
        mine = pl.multiple_of(me * 8, 8)
        size = GROUPS[g][1]
        for tz, tx in peers:
            there = pl.multiple_of((zs * tx + tz) * 8, 8)
            pltpu.make_async_remote_copy(
                src_ref=src[g].at[pl.ds(there, size), :], dst_ref=dst[g].at[pl.ds(mine, size), :],
                send_sem=send.at[n, g], recv_sem=recv.at[n, g],
                device_id={"gz": tz, "gx": tx}, device_id_type=MESH,
            ).start()
        dst[g][pl.ds(mine, 8), :] = src[g][pl.ds(mine, 8), :]

    def all_wait(ref, sem, n, g):
        part = ref[g].at[pl.ds(0, GROUPS[g][1] * (total - 1)), :]
        pltpu.make_async_copy(part, part, sem.at[n, g]).wait()

    def gathered(ref, g):
        return [ref[g][pl.ds(c, 128, stride=8), :] for c in range(GROUPS[g][1])]

    def scatter(ref, g, value):
        for c in range(GROUPS[g][1]):
            ref[g][pl.ds(c, 128, stride=8), :] = value[:, 128 * c : 128 * c + 128]

    for g in range(2):
        z_send(s1, r1, 0, g, [to for to, _ in z_peers])
    for g in range(2):
        r1[g][j] = s1[g][j]
    for to in x_peers:
        pl.semaphore_signal(ready, inc=1, device_id={"gz": j, "gx": to}, device_id_type=MESH)
    scale = -1.0 / (1024.0 * 1024.0)
    half = scale * 0.5 / shear_ref
    couple = scale * (lame_ref + shear_ref) / (shear_ref * (lame_ref + 2.0 * shear_ref))
    for k, value in enumerate(green_maps(8 * me)):
        maps[k] = value
    for copy in loads[5:]:
        copy.wait()

    def table(ref):
        return ref[...]

    def forward(g):
        block = z_forward(lambda a, b: r1[g][a, b], table(twz_ref), range(GROUPS[g][1]))
        scatter(s2, g, mul(table(left_ref), split3(block, 1), 1, 1))

    def across(g):
        tabs = [table(ref) for ref in (left_ref, right_ref, fwd_ref, inv_ref, twz_ref, twx_ref, both_ref)]
        wide = jnp.concatenate(gathered(r2, g), axis=1)
        scatter(s3, g, middle(wide, [maps[k] for k in range(4)], half, couple, tabs))

    def backward(g):
        flat = jnp.concatenate([w.T for w in gathered(r3, g)], axis=0)
        parts = mul(split3(flat, 1), table(right_ref))
        for c in range(GROUPS[g][1]):
            tiles = z_inverse(parts[128 * c : 128 * c + 128], table(twz_ref))
            for k in range(8):
                s4[g][k, 2 * c] = tiles[k][0]
                s4[g][k, 2 * c + 1] = tiles[k][1]

    for g in range(2):
        z_wait(r1, recv, 0, g)
        forward(g)
        if g == 0:
            pl.semaphore_wait(ready, xs - 1)
        all_send(s2, r2, 1, g, [peer(*o) for o in everyone])
    for g in range(2):
        all_wait(r2, recv, 1, g)
        across(g)
        all_send(s3, r3, 2, g, early_rows)
    for g in range(2):
        all_wait(r3, recv, 2, g)
        backward(g)
        z_send(s4, r4, 3, g, early_first)
        r4[g][j] = s4[g][j]

    for g in range(2):
        z_wait(s1, send, 0, g)
        all_wait(s2, send, 1, g)
        all_wait(s3, send, 2, g)

    def arrived(slot, s):
        return jnp.concatenate([r4[slot // 3][k, 2 * (slot % 3) + s] for k in range(8)], axis=0) + mean[COMPS[slot]]

    for g, (first, size) in enumerate(GROUPS):
        z_wait(r4, recv, 3, g)
        for s in range(2):
            e = [jnp.full((64, 128), mean[1], jnp.float32)] * 6
            for slot in range(first, first + size):
                e[COMPS[slot]] = arrived(slot, s)
            lam, mu2, stiff = (cells[s, k] for k in range(3))
            stress = law(e, lam, mu2, stiff, [cells[s, k] for k in range(3, 6)])
            done = [COMPS[k] for k in range(first, first + size)] + [1] * (g == 0)
            for c in done:
                strain_out[c, s] = e[c]
                stress_out[c, s] = stress[c]

    for g in range(2):
        z_wait(s4, send, 3, g)


def put_out(strain, stress, strain_hbm, stress_hbm, sem):
    copies = []
    size = 6 // PARTS
    for k in range(PARTS):
        part = pl.ds(size * k, size)
        for n, (src, dst) in enumerate(((strain, strain_hbm), (stress, stress_hbm))):
            copies.append(pltpu.make_async_copy(src.at[part], dst.at[part], sem.at[n, k]))
    for copy in copies:
        copy.start()
    for copy in copies:
        copy.wait()


def solution(mesh):
    consts = tables()

    def shards(strain, labels, normals, moduli, mean_strain):
        vmem = pl.BlockSpec(memory_space=pltpu.VMEM)
        away = pl.BlockSpec(memory_space=pl.ANY)
        arrays = [strain, labels, normals, moduli, mean_strain] + [jnp.asarray(a) for a in consts]
        tiles = [pltpu.VMEM((8, 2 * n, 8, 128), jnp.float32) for _, n in GROUPS]
        wide = [pltpu.VMEM((1024, 128), jnp.float32)] * 2
        fields = pl.pallas_call(
            kernel,
            out_shape=[pltpu.VMEM(strain.shape, jnp.float32)] * 2,
            in_specs=[away] * len(arrays),
            out_specs=[vmem, vmem],
            scratch_shapes=[(pltpu.SMEM if a.ndim == 1 else pltpu.VMEM)(a.shape, a.dtype) for a in arrays]
            + tiles * 2 + wide * 4 + tiles * 2
            + [pltpu.VMEM((2, 6, 64, 128), jnp.float32), pltpu.VMEM((4, 128, 128), jnp.float32)]
            + [pltpu.SemaphoreType.DMA((len(arrays),)), pltpu.SemaphoreType.DMA((4, 2))]
            + [pltpu.SemaphoreType.DMA((4, 2)), pltpu.SemaphoreType.REGULAR],
            compiler_params=pltpu.CompilerParams(collective_id=0, has_side_effects=True),
        )(*arrays)
        return tuple(
            pl.pallas_call(
                put_out,
                out_shape=[jax.ShapeDtypeStruct(strain.shape, jnp.float32)] * 2,
                in_specs=[vmem] * 2,
                out_specs=[away] * 2,
                scratch_shapes=[pltpu.SemaphoreType.DMA((2, PARTS))],
            )(*[pltpu.with_memory_space_constraint(a, pltpu.VMEM) for a in fields])
        )

    in_specs = (P(None, None, "gx", "gz"), P(None, "gx", "gz"), P(None, "gx", "gz"), P(), P())
    out_specs = (P(None, None, "gx", "gz"), P(None, None, "gx", "gz"))
    return jax.shard_map(shards, mesh=mesh, in_specs=in_specs, out_specs=out_specs, check_vma=False)
```

```python
import itertools
import math

import jax
import jax.numpy as jnp
import numpy as np
from jax import lax
from jax.experimental import pallas as pl
from jax.experimental.pallas import tpu as pltpu
from jax.sharding import PartitionSpec as P

ANGLES = 8
BLK = 16
PARTS = 1
COMPS = (0, 2, 4, 3, 5)
GROUPS = ((0, 3), (3, 2))
MESH = pl.DeviceIdType.MESH
HIGH = lax.Precision.HIGHEST
ROOT = math.sqrt(0.5)


def tables():
    k = np.arange(128)
    w = 2.0 * np.pi / 128.0 * (k[:, None] * k[None, :] % 128)
    dft = np.concatenate([np.cos(w), np.sin(w)], axis=1)
    r = np.arange(8)
    wz = 2.0 * np.pi / 1024.0 * (r[:, None] * k[None, :])
    twz = np.concatenate([np.cos(wz), np.sin(wz)], axis=0)
    lane = np.arange(128)
    t, low = lane // 64, lane % 8
    wx = 2.0 * np.pi / 1024.0 * (k[:, None] * low[None, :])
    sign = np.where(t == 0, 1.0, -1.0)[None, :]
    twx = np.concatenate([np.cos(wx), np.sin(wx) * sign], axis=0)
    same = (lane // 8 % 8)[:, None] == (lane // 8 % 8)[None, :]
    w8 = 2.0 * np.pi / 8.0 * (low[:, None] * low[None, :] % 8)
    ta, tb = t[:, None], t[None, :]
    cos8, sin8 = np.cos(w8) * same, np.sin(w8) * same
    fwd = np.where(ta == tb, cos8, np.where(ta == 1, sin8, -sin8))
    inv = np.where(ta == tb, cos8, np.where(ta == 1, -sin8, sin8))
    fwd2 = np.concatenate([fwd, np.roll(fwd, 64, axis=0)], axis=0)
    inv2 = np.concatenate([inv, np.roll(inv, 64, axis=1)], axis=1)
    twz, twx = np.asarray(twz, np.float32), np.asarray(twx, np.float32)
    stacked = np.concatenate([np.cos(w), np.sin(w)], axis=0)
    return [left_table(dft), right_table(dft), right_table(fwd2), right_table(inv2), twz, twx, left_table(stacked)]


def halves(a):
    a = np.asarray(a, np.float32)
    high = a.astype(jnp.bfloat16)
    return high, (a - high.astype(np.float32)).astype(jnp.bfloat16)


def left_table(a):
    high, low = halves(a)
    return np.concatenate([high, low, high], axis=1)


def right_table(a):
    high, low = halves(a)
    return np.concatenate([high, low, high], axis=0)


def split3(x, axis):
    high = x.astype(jnp.bfloat16)
    low = (x - high.astype(jnp.float32)).astype(jnp.bfloat16)
    return jnp.concatenate([high, high, low], axis=axis)


def mul(a, b, ca=1, cb=0):
    return lax.dot_general(a, b, (((ca,), (cb,)), ((), ())), preferred_element_type=jnp.float32)


def dot(a, b):
    return lax.dot_general(
        a, b, (((1,), (0,)), ((), ())), precision=HIGH, preferred_element_type=jnp.float32
    )


def fft8(u, sign):
    def add(a, b):
        return (a[0] + b[0], a[1] + b[1])

    def sub(a, b):
        return (a[0] - b[0], a[1] - b[1])

    def turn(a):
        return (-a[1], a[0]) if sign > 0 else (a[1], -a[0])

    def fft4(v):
        e, f = add(v[0], v[2]), sub(v[0], v[2])
        g, h = add(v[1], v[3]), turn(sub(v[1], v[3]))
        return [add(e, g), add(f, h), sub(e, g), sub(f, h)]

    even, odd = fft4(u[0::2]), fft4(u[1::2])
    o1, o3 = odd[1], odd[3]
    t1, t3 = turn(o1), turn(o3)
    odd = [
        odd[0],
        ((o1[0] + t1[0]) * ROOT, (o1[1] + t1[1]) * ROOT),
        turn(odd[2]),
        ((t3[0] - o3[0]) * ROOT, (t3[1] - o3[1]) * ROOT),
    ]
    return [add(even[k], odd[k]) for k in range(4)] + [sub(even[k], odd[k]) for k in range(4)]


def z_forward(load, twz, slots):
    blocks = []
    for c in slots:
        u = fft8([(load(j, 2 * c), load(j, 2 * c + 1)) for j in range(8)], -1)
        real, imag = [], []
        for r in range(8):
            re, im = u[r]
            if r:
                co, si = twz[r : r + 1, :], twz[8 + r : 9 + r, :]
                re, im = re * co + im * si, im * co - re * si
            real.append(re)
            imag.append(im)
        re, im = jnp.concatenate(real, axis=0), jnp.concatenate(imag, axis=0)
        left = jnp.concatenate([re, im], axis=0)
        right = jnp.concatenate([im, -re], axis=0)
        blocks.append(jnp.concatenate([left, right], axis=1))
    return jnp.concatenate(blocks, axis=0)


def z_inverse(parts, twz):
    v = []
    for r in range(8):
        lo, hi = slice(8 * r, 8 * r + 8), slice(64 + 8 * r, 72 + 8 * r)
        re = parts[lo, :128] - parts[hi, 128:]
        im = parts[hi, :128] + parts[lo, 128:]
        if r:
            co, si = twz[r : r + 1, :], twz[8 + r : 9 + r, :]
            re, im = re * co - im * si, im * co + re * si
        v.append((re, im))
    return fft8(v, 1)


def green_maps(kz_base):
    row = lax.broadcasted_iota(jnp.int32, (128, 128), 0)
    lane = lax.broadcasted_iota(jnp.int32, (128, 128), 1)
    kx = row + 128 * (lane % 8)
    kz = kz_base + lane // 8 % 8
    fx = jnp.where(kx < 512, kx, kx - 1024).astype(jnp.float32)
    fz = jnp.where(kz < 512, kz, kz - 1024).astype(jnp.float32)
    xx, zz, xz = fx * fx, fz * fz, fx * fz
    size = xx + zz
    inv = 1.0 / jnp.where(size == 0.0, 1.0, size)
    p, q, r = xx * inv, zz * inv, xz * inv
    return p, q, jnp.where((kx == 512) != (kz == 512), 0.0, r), p * q


def green(spec, maps, half, couple):
    p, q, r, pq = maps
    if len(spec) == 2:
        s3, s5 = spec
        return half * (s5 * r + s3 * q), half * (s5 * p + s3 * r)
    s0, s2, s4 = spec
    even, cross = s0 * p + s2 * q, s4 * r
    load = couple * (even + 2.0 * cross)
    return (
        2.0 * half * (s0 * p + cross) - load * p,
        2.0 * half * (s2 * q + cross) - load * q,
        half * (r * (s0 + s2) + s4 * (p + q)) - couple * (r * even + 2.0 * (s4 * pq)),
    )


def middle(wide, maps, half, couple, tabs):
    left, _, fwd, inv, _, twx, both_left = tabs
    n = wide.shape[1] // 128
    lane = lax.broadcasted_iota(jnp.int32, (128, 128), 1)
    sign = jnp.where(lane < 64, 1.0, -1.0)
    cx, sx = twx[:128, :], twx[128:, :]

    def lanes(x, c):
        return x[:, 128 * c : 128 * c + 128]

    def rows(x, c):
        return x[128 * c : 128 * c + 128]

    cs = mul(both_left, split3(wide, 0))
    turned = []
    for c in range(n):
        v, u = lanes(cs[:128], c), -(lanes(cs[128:], c) * sign)
        turned.append(jnp.concatenate([v * cx + u * sx, u * cx - v * sx], axis=1))
    spec = mul(split3(jnp.concatenate(turned, axis=0), 1), fwd)
    new = green([rows(spec, c) for c in range(n)], maps, half, couple)
    both = mul(split3(jnp.concatenate(new, axis=0), 1), inv)
    out = []
    for c in range(n):
        y, ry = rows(both, c)[:, :128], rows(both, c)[:, 128:]
        out.append(jnp.concatenate([y * cx - ry * sx, -((ry * cx + y * sx) * sign)], axis=0))
    return mul(left, split3(jnp.concatenate(out, axis=1), 0))


def stress_terms(moduli, labels):
    lam = jnp.where(labels == 1, moduli[2], moduli[0])
    mu = jnp.where(labels == 1, moduli[3], moduli[1])
    stiff = moduli[4] * labels.astype(jnp.float32)
    return lam, mu, stiff


def orient(normals, s):
    steps = normals.astype(jnp.float32)
    rows = lax.broadcasted_iota(jnp.int32, (64, 4), 0) // BLK == lax.broadcasted_iota(jnp.int32, (64, 4), 1)
    cols = lax.broadcasted_iota(jnp.int32, (8, 128), 0) == lax.broadcasted_iota(jnp.int32, (8, 128), 1) // BLK
    wide = dot(dot(rows.astype(jnp.float32), steps), cols.astype(jnp.float32))
    cosine, sine = jnp.ones_like(wide), jnp.zeros_like(wide)
    for k in range(1, ANGLES):
        here = jnp.abs(wide - k) < 0.5
        cosine = jnp.where(here, math.cos(math.pi / ANGLES * k), cosine)
        sine = jnp.where(here, math.sin(math.pi / ANGLES * k), sine)
    return cosine * cosine, sine * sine, cosine * sine


def law(e, lam, mu2, stiff, angle):
    cc, ss, cs = angle
    trace = lam * (e[0] + e[1] + e[2])
    normal = stiff * (cc * e[0] + ss * e[2] + 2.0 * cs * e[4])
    dyad = (cc, None, ss, None, cs, None)
    out = []
    for k in range(6):
        value = mu2 * e[k]
        if k < 3:
            value = value + trace
        if dyad[k] is not None:
            value = value + normal * dyad[k]
        out.append(value)
    return out


def far_first(sizes, hops):
    offsets = [o for o in itertools.product(*[range(n) for n in sizes]) if any(o)]
    return sorted(offsets, key=lambda o: -sum(h(v) for h, v in zip(hops, o)))


def ring(v):
    return min(v, 4 - v)


def kernel(
    strain_hbm, labels_hbm, normals_hbm, moduli_hbm, mean_hbm, left_hbm, right_hbm, fwd_hbm, inv_hbm, twz_hbm, twx_hbm, both_hbm,
    strain_out, stress_out,
    strain, labels, normals, moduli, mean, left_ref, right_ref, fwd_ref, inv_ref, twz_ref, twx_ref, both_ref,
    *rest,
):
    s1, r1, s2, r2, s3, r3, s4, r4 = (rest[2 * k : 2 * k + 2] for k in range(8))
    cells, maps, load, send, recv, ready = rest[16:]
    zs, xs = lax.axis_size("gz"), lax.axis_size("gx")
    zs_stride = xs
    total = zs * xs
    j = lax.axis_index("gz")
    i = lax.axis_index("gx")
    barrier = pltpu.get_barrier_semaphore()
    for k in (5, 3, 4, 1, 7, 2, 6):
        pl.semaphore_signal(barrier, inc=1, device_id={"gz": lax.rem(j + k, zs), "gx": i}, device_id_type=MESH)
    for k in (10, 6, 8, 11, 9, 7, 5, 12, 4, 13, 3, 14, 2, 15, 1):
        pl.semaphore_signal(barrier, inc=1, device_id={"gz": j, "gx": lax.rem(i + k, xs)}, device_id_type=MESH)

    loads = [
        pltpu.make_async_copy(a, b, load.at[k])
        for k, (a, b) in enumerate((
            (strain_hbm, strain), (labels_hbm, labels), (normals_hbm, normals), (moduli_hbm, moduli),
            (mean_hbm, mean), (twz_hbm, twz_ref),
            (left_hbm, left_ref), (twx_hbm, twx_ref), (fwd_hbm, fwd_ref), (inv_hbm, inv_ref), (right_hbm, right_ref),
            (both_hbm, both_ref),
        ))
    ]
    for copy in loads:
        copy.start()
    me = zs * i + j
    z, x, core = j // 2, i // 4, lax.rem(i, 2)
    y = 2 * lax.rem(j, 2) + lax.rem(i // 2, 2)

    px = [4 * lax.rem(x + d, 4) for d in range(4)]
    py = [lax.rem(y + d, 4) for d in range(4)]
    pz = [2 * lax.rem(z + d, 4) for d in range(4)]
    pc = [lax.rem(core + d, 2) for d in range(2)]
    high, low = [v // 2 for v in py], [2 * lax.rem(v, 2) for v in py]

    def peer(dx, dy, dz, dc):
        return pz[dz] + high[dy], px[dx] + low[dy] + pc[dc]

    z_peers = [peer(0, dy, dz, 0) for dz, dy in far_first((4, 3), (ring, ring)) if dy != 1]
    early_first = [k + (k - j + zs) // zs for k in range(zs - 1)]
    everyone = far_first((4, 4, 4, 2), (ring, ring, ring, lambda v: 0))

    def named(tz, tx):
        return zs_stride * tz + tx, 8 * (zs * tx + tz)

    columns = {(dx, dy): named(high[dy], px[dx] + low[dy]) for dx in range(4) for dy in range(4)}
    stacks = {(dz, dc): named(pz[dz], pc[dc]) for dz in range(4) for dc in range(2)}

    def both(a, b):
        return a[0] + b[0], a[1] + b[1]

    everyone = [both(columns[o[:2]], stacks[o[2:]]) for o in everyone]

    row = 2 * x + lax.rem(y, 2)
    early_rows = []
    for k, (rx, ry) in enumerate(itertools.product(range(4), range(2))):
        for dz, dy, dc in far_first((4, 2, 2), (ring, lambda v: 2 * v, lambda v: 0)):
            early_rows.append(both(named(lax.rem(y // 2 + dy, 2), 4 * rx + 2 * ry), stacks[dz, dc]))
        if k < 7:
            other = k + (k - row + 8) // 8
            early_rows.append(named(j, 2 * other + core))

    def x_index(dx, dy, dc):
        low = lax.rem(i // 2 + dy, 2)
        return 4 * lax.rem(x + dx, 4) + 2 * low + lax.rem(core + dc, 2)

    x_peers = [x_index(*o) for o in far_first((4, 2, 2), (ring, lambda v: v, lambda v: 0))]

    for copy in loads[:5]:
        copy.wait()

    m = [moduli[k] for k in range(5)]
    lame_ref = 0.5 * (m[0] + m[2])
    shear_ref = 0.5 * (m[1] + m[3])
    for s in range(2):
        angle = orient(normals[s], s)
        lam, mu, stiff = stress_terms(m, labels[s])
        e = [strain[c, s] for c in range(6)]
        pol = law(e, lam - lame_ref, 2.0 * (mu - shear_ref), stiff, angle)
        for slot, c in enumerate(COMPS):
            for g in range(8):
                s1[slot // 3][g, 2 * (slot % 3) + s] = pol[c][8 * g : 8 * g + 8, :]
        for k, value in enumerate((lam, 2.0 * mu, stiff, *angle)):
            cells[s, k] = value

    pl.semaphore_wait(barrier, zs + xs - 2)

    def z_send(src, dst, n, g, peers):
        for to in peers:
            pltpu.make_async_remote_copy(
                src_ref=src[g].at[to], dst_ref=dst[g].at[j], send_sem=send.at[n, g], recv_sem=recv.at[n, g],
                device_id={"gz": to, "gx": i}, device_id_type=MESH,
            ).start()

    def z_wait(ref, sem, n, g):
        part = ref[g].at[pl.ds(0, zs - 1)]
        pltpu.make_async_copy(part, part, sem.at[n, g]).wait()

    def all_send(src, dst, n, g, peers):
        mine = pl.multiple_of(me * 8, 8)
        size = GROUPS[g][1]
        for to, there in peers:
            there = pl.multiple_of(there, 8)
            pltpu.make_async_remote_copy(
                src_ref=src[g].at[pl.ds(there, size), :], dst_ref=dst[g].at[pl.ds(mine, size), :],
                send_sem=send.at[n, g], recv_sem=recv.at[n, g],
                device_id=to, device_id_type=pl.DeviceIdType.LOGICAL,
            ).start()
        dst[g][pl.ds(mine, 8), :] = src[g][pl.ds(mine, 8), :]

    def all_wait(ref, sem, n, g):
        part = ref[g].at[pl.ds(0, GROUPS[g][1] * (total - 1)), :]
        pltpu.make_async_copy(part, part, sem.at[n, g]).wait()

    def gathered(ref, g):
        return [ref[g][pl.ds(c, 128, stride=8), :] for c in range(GROUPS[g][1])]

    def scatter(ref, g, value):
        for c in range(GROUPS[g][1]):
            ref[g][pl.ds(c, 128, stride=8), :] = value[:, 128 * c : 128 * c + 128]

    for g in range(2):
        z_send(s1, r1, 0, g, [to for to, _ in z_peers])
    for g in range(2):
        r1[g][j] = s1[g][j]
    for to in x_peers:
        pl.semaphore_signal(ready, inc=1, device_id={"gz": j, "gx": to}, device_id_type=MESH)
    scale = -1.0 / (1024.0 * 1024.0)
    half = scale * 0.5 / shear_ref
    couple = scale * (lame_ref + shear_ref) / (shear_ref * (lame_ref + 2.0 * shear_ref))
    for k, value in enumerate(green_maps(8 * me)):
        maps[k] = value
    for copy in loads[5:]:
        copy.wait()

    def table(ref):
        return ref[...]

    def forward(g):
        block = z_forward(lambda a, b: r1[g][a, b], table(twz_ref), range(GROUPS[g][1]))
        scatter(s2, g, mul(table(left_ref), split3(block, 1), 1, 1))

    def across(g):
        tabs = [table(ref) for ref in (left_ref, right_ref, fwd_ref, inv_ref, twz_ref, twx_ref, both_ref)]
        wide = jnp.concatenate(gathered(r2, g), axis=1)
        scatter(s3, g, middle(wide, [maps[k] for k in range(4)], half, couple, tabs))

    def backward(g):
        flat = jnp.concatenate([w.T for w in gathered(r3, g)], axis=0)
        parts = mul(split3(flat, 1), table(right_ref))
        for c in range(GROUPS[g][1]):
            tiles = z_inverse(parts[128 * c : 128 * c + 128], table(twz_ref))
            for k in range(8):
                s4[g][k, 2 * c] = tiles[k][0]
                s4[g][k, 2 * c + 1] = tiles[k][1]

    for g in range(2):
        z_wait(r1, recv, 0, g)
        forward(g)
        if g == 0:
            pl.semaphore_wait(ready, xs - 1)
        all_send(s2, r2, 1, g, everyone)
    for g in range(2):
        all_wait(r2, recv, 1, g)
        across(g)
        all_send(s3, r3, 2, g, early_rows)
    for g in range(2):
        all_wait(r3, recv, 2, g)
        backward(g)
        z_send(s4, r4, 3, g, early_first)
        r4[g][j] = s4[g][j]

    for g in range(2):
        z_wait(s1, send, 0, g)
        all_wait(s2, send, 1, g)
        all_wait(s3, send, 2, g)

    def arrived(slot, s):
        return jnp.concatenate([r4[slot // 3][k, 2 * (slot % 3) + s] for k in range(8)], axis=0) + mean[COMPS[slot]]

    for g, (first, size) in enumerate(GROUPS):
        z_wait(r4, recv, 3, g)
        for s in range(2):
            e = [jnp.full((64, 128), mean[1], jnp.float32)] * 6
            for slot in range(first, first + size):
                e[COMPS[slot]] = arrived(slot, s)
            lam, mu2, stiff = (cells[s, k] for k in range(3))
            stress = law(e, lam, mu2, stiff, [cells[s, k] for k in range(3, 6)])
            done = [COMPS[k] for k in range(first, first + size)] + [1] * (g == 0)
            for c in done:
                strain_out[c, s] = e[c]
                stress_out[c, s] = stress[c]

    for g in range(2):
        z_wait(s4, send, 3, g)


def put_out(strain, stress, strain_hbm, stress_hbm, sem):
    copies = []
    size = 6 // PARTS
    for k in range(PARTS):
        part = pl.ds(size * k, size)
        for n, (src, dst) in enumerate(((strain, strain_hbm), (stress, stress_hbm))):
            copies.append(pltpu.make_async_copy(src.at[part], dst.at[part], sem.at[n, k]))
    for copy in copies:
        copy.start()
    for copy in copies:
        copy.wait()


def solution(mesh):
    consts = tables()

    def shards(strain, labels, normals, moduli, mean_strain):
        vmem = pl.BlockSpec(memory_space=pltpu.VMEM)
        away = pl.BlockSpec(memory_space=pl.ANY)
        arrays = [strain, labels, normals, moduli, mean_strain] + [jnp.asarray(a) for a in consts]
        tiles = [pltpu.VMEM((8, 2 * n, 8, 128), jnp.float32) for _, n in GROUPS]
        wide = [pltpu.VMEM((1024, 128), jnp.float32)] * 2
        fields = pl.pallas_call(
            kernel,
            out_shape=[pltpu.VMEM(strain.shape, jnp.float32)] * 2,
            in_specs=[away] * len(arrays),
            out_specs=[vmem, vmem],
            scratch_shapes=[(pltpu.SMEM if a.ndim == 1 else pltpu.VMEM)(a.shape, a.dtype) for a in arrays]
            + tiles * 2 + wide * 4 + tiles * 2
            + [pltpu.VMEM((2, 6, 64, 128), jnp.float32), pltpu.VMEM((4, 128, 128), jnp.float32)]
            + [pltpu.SemaphoreType.DMA((len(arrays),)), pltpu.SemaphoreType.DMA((4, 2))]
            + [pltpu.SemaphoreType.DMA((4, 2)), pltpu.SemaphoreType.REGULAR],
            compiler_params=pltpu.CompilerParams(collective_id=0, has_side_effects=True),
        )(*arrays)
        return tuple(
            pl.pallas_call(
                put_out,
                out_shape=[jax.ShapeDtypeStruct(strain.shape, jnp.float32)] * 2,
                in_specs=[vmem] * 2,
                out_specs=[away] * 2,
                scratch_shapes=[pltpu.SemaphoreType.DMA((2, PARTS))],
            )(*[pltpu.with_memory_space_constraint(a, pltpu.VMEM) for a in fields])
        )

    in_specs = (P(None, None, "gx", "gz"), P(None, "gx", "gz"), P(None, "gx", "gz"), P(), P())
    out_specs = (P(None, None, "gx", "gz"), P(None, None, "gx", "gz"))
    return jax.shard_map(shards, mesh=mesh, in_specs=in_specs, out_specs=out_specs, check_vma=False)
```
